128 devices in a mesh: seq: 16 (over z, x), exp: 8 (over y, core).
Axes of the slice: x: 4, y: 4, z: 4, core: 2. Of those that a mesh axis runs over, the one named last changes fastest.
Arguments:
- residual: bfloat16 [8, 2048, 2048], P('exp', 'seq'), may hold values from -0.59765625 to 0.59765625
- query_heads: bfloat16 [8, 2048, 2048], P('exp', 'seq'), may hold values from -8 to 8
- key_heads: bfloat16 [8, 2048, 2048], P('exp', 'seq'), may hold values from -8 to 8
- value_heads: bfloat16 [8, 2048, 2048], P('exp', 'seq'), may hold values from -6 to 6
- segment_ids: int32 [8, 2048], P('exp'), may hold values from 0 to 15, never falling along the last dimension, each value on 1 to 512 neighbouring positions
- w_out: bfloat16 [2048, 2048], replicated, may hold values from -0.125 to 0.125
- norm_gain: float32 [2048], replicated, may hold values from 0.5 to 1.5
- gate_scores: float32 [8, 2048, 6], P('exp', 'seq'), may hold values from -8 to 260
- routes: int32 [8, 2048, 6], P('exp', 'seq'), may hold values from 0 to 63, as said below
- w_gate: bfloat16 [128, 2048, 704], P(('seq', 'exp')), may hold values from -0.125 to 0.125
- w_up: bfloat16 [128, 2048, 704], P(('seq', 'exp')), may hold values from -0.125 to 0.125
- w_down: bfloat16 [128, 704, 2048], P(('seq', 'exp')), may hold values from -0.3125 to 0.3125
- page_holder: int32 [8, 128], replicated, may hold values from 0 to 7, as said below
- page_slot: int32 [8, 128], replicated, may hold values from 0 to 15, as said below
Outputs:
- layer_out: bfloat16 [8, 2048, 2048], P('exp', 'seq')
- kv_cache: bfloat16 [16, 128, 16, 4096], P('seq', 'exp')
The draws below stay inside these ranges and needn't reach their ends.
Inputs may be any that keep to these rules, and one draw needn't show every extreme that they name: `routes`: each token names 6 different experts; among the 128 rows of one device every expert is named either exactly 16 times or not at all, and one expert is named exactly 16 times among the rows of every device. `segment_ids`: A document never falls back; one document holds at most 512 tokens. `page_holder`: of the 8 pages of one device's tokens, at most 2 go to one holder, and for every seq block one holder receives exactly 2 pages from every pack. `page_slot`: pages of one seq block that go to the same holder have distinct slots.
All inputs are finite; a program needn't handle non-finite values.
Results may differ from the reference program's by a relative error of at most 0.015.
Values may be sent and summed in bfloat16 or wider, within the bound.
A program may use at most 128 MiB of HBM per device.

```python
import math
import jax
import jax.numpy as jnp
import numpy as np
from jax import lax

D = 2048
H = 16
HD = 128
FF = 1408
TOP = 6
TOK_DEV = 128
PAGE = 16
SEND_CAP = 2
DOCS = 16
EXPERTS = 64
PACKS = 8
LENGTH = 2048
CAP = 16
PAGES = 128
PAGES_DEV = 8
SLOTS = 16
N_SEQ = 16


def drawn_field(key):
    return jnp.clip(jax.random.normal(key, (PACKS, LENGTH, H * HD), jnp.float32), -6.0, 6.0)


def draw_query_heads(key, part):
    field = drawn_field(jax.random.fold_in(key, 1))
    return field.astype(jnp.bfloat16)


def draw_key_heads(key, part):
    field = drawn_field(jax.random.fold_in(key, 2))
    return field.astype(jnp.bfloat16)


def random_order(key, shape):
    count = shape[-1]
    scores = jax.random.randint(key, shape, 0, 1 << 20) * count + jnp.arange(count, dtype=jnp.int32)
    return jnp.argsort(scores, axis=-1).astype(jnp.int32)


def route_plan(key):
    base = jax.random.fold_in(key, 31)
    pop_key, pick_key, token_key, column_key, flag_key, mixed_key = jax.random.split(base, 6)
    blocks = PACKS * LENGTH // TOK_DEV
    groups = TOK_DEV // CAP
    active = TOP * groups
    popularity = random_order(pop_key, (EXPERTS,))
    favourite = (popularity == EXPERTS - 1).astype(jnp.int32) * (8 * EXPERTS)
    pick_scores = jax.random.randint(pick_key, (blocks, EXPERTS), 0, 4 * EXPERTS) + 2 * popularity[None, :] + favourite[None, :]
    pick_scores = pick_scores * EXPERTS + jnp.arange(EXPERTS, dtype=jnp.int32)[None, :]
    _, picked = lax.top_k(pick_scores, active)
    set_experts = picked.astype(jnp.int32).reshape(blocks, TOP, groups)
    token_order = random_order(token_key, (blocks, TOP, TOK_DEV))
    by_set = jnp.take_along_axis(set_experts, token_order // CAP, axis=2)
    base_routes = jnp.transpose(by_set, (0, 2, 1))
    column_order = random_order(column_key, (blocks, TOK_DEV, TOP))
    routes = jnp.take_along_axis(base_routes, column_order, axis=2)
    structured = jax.random.randint(flag_key, (blocks, 1, 1), 0, 4) != 0
    mixed_order = random_order(mixed_key, (blocks, TOK_DEV, TOP))
    top_mask = jnp.where(structured, column_order < TOP // 2, mixed_order < TOP // 2)
    return (routes.reshape(PACKS, LENGTH, TOP).astype(jnp.int32), top_mask.reshape(PACKS, LENGTH, TOP))


def draw_routes(key, part):
    routes, top_mask = route_plan(key)
    return routes


def draw_gate_scores(key, part):
    shape = (PACKS, LENGTH, TOP)
    routes, top_mask = route_plan(key)
    base = jax.random.fold_in(key, 5)
    row_key, top_key, small_key = jax.random.split(base, 3)
    top_jitter = jax.random.uniform(top_key, shape, jnp.float32, 0.0, 0.1)
    small_jitter = jax.random.uniform(small_key, shape, jnp.float32, 0.0, 0.05)
    row_level = jnp.clip(2.0 * jax.random.normal(row_key, (PACKS, LENGTH, 1), jnp.float32), -4.0, 8.0)
    return jnp.where(top_mask, row_level + top_jitter, row_level - 3.1 - small_jitter)


def page_tables(key):
    base = jax.random.fold_in(key, 23)
    hot_key, score_key, shuffle_key, slot_key = jax.random.split(base, 4)
    blocks = LENGTH // TOK_DEV
    holders = PACKS
    spare = PAGES_DEV - SEND_CAP
    width_cand = (holders - 1) * SEND_CAP
    hot = jax.random.randint(hot_key, (blocks,), 0, holders)
    order = jnp.arange(width_cand, dtype=jnp.int32) // SEND_CAP
    candidates = (hot[None, :, None] + 1 + order[None, None, :]) % holders
    candidates = jnp.broadcast_to(candidates, (PACKS, blocks, width_cand))
    bias = (holders - 1 - order) * 2
    scores = jax.random.randint(score_key, (PACKS, blocks, width_cand), 0, 16) + bias
    scores = scores * width_cand + jnp.arange(width_cand, dtype=jnp.int32)
    _, picked = lax.top_k(scores, spare)
    chosen_holders = jnp.take_along_axis(candidates, picked, axis=-1)
    hot_part = jnp.broadcast_to(hot[None, :, None], (PACKS, blocks, SEND_CAP))
    listing = jnp.concatenate([hot_part, chosen_holders], axis=-1)
    shuffle = jax.random.randint(shuffle_key, (PACKS, blocks, PAGES_DEV), 0, 1 << 20) * PAGES_DEV + jnp.arange(PAGES_DEV, dtype=jnp.int32)
    permuted = jnp.argsort(shuffle, axis=-1)
    holder = jnp.take_along_axis(listing, permuted, axis=-1)
    flat = jnp.transpose(holder, (1, 0, 2)).reshape(blocks, PACKS * PAGES_DEV)
    holder_hits = (flat[:, :, None] == jnp.arange(holders, dtype=jnp.int32)).astype(jnp.int32)
    arrival = jnp.sum((jnp.cumsum(holder_hits, axis=1) - 1) * holder_hits, axis=-1)
    slot_total = holders * SEND_CAP
    slot_scores = jax.random.randint(slot_key, (blocks, holders, slot_total), 0, 1 << 20) * slot_total + jnp.arange(slot_total, dtype=jnp.int32)
    slot_order = jnp.argsort(slot_scores, axis=-1).reshape(blocks, holders * slot_total)
    slot_flat = jnp.take_along_axis(slot_order, flat * slot_total + arrival, axis=1)
    slot = jnp.transpose(slot_flat.reshape(blocks, PACKS, PAGES_DEV), (1, 0, 2)).reshape(PACKS, blocks * PAGES_DEV)
    return (holder.reshape(PACKS, blocks * PAGES_DEV).astype(jnp.int32), slot.astype(jnp.int32))


def draw_page_holder(key, part):
    holder, slot = page_tables(key)
    return holder


def draw_page_slot(key, part):
    holder, slot = page_tables(key)
    return slot


def shard_levels(key, dims, cuts, smallest, high):
    level, own = 1.0, jax.random.fold_in(key, 6)
    for axis_at, parts in cuts:
        heights = jnp.exp(jax.random.uniform(jax.random.fold_in(own, axis_at), (parts,), jnp.float32, smallest / len(cuts), high / len(cuts)))
        level = level * jnp.repeat(heights, dims[axis_at] // parts).reshape([-1 if axis == axis_at else 1 for axis in range(len(dims))])
    return level


def length_profile(count, total, reach, skew):
    weights = [(1 << 20) // math.isqrt(rank ** skew) + 1 for rank in range(2, count + 1)]
    surplus, counts = total - reach - (count - 1), [1] * (count - 1)
    while surplus > 0:
        free = [i for i in range(count - 1) if counts[i] < reach]
        whole, remaining = sum([weights[i] for i in free]), surplus
        for i in free:
            addition = min(reach - counts[i], max(1, remaining * weights[i] // whole), surplus)
            counts[i] = counts[i] + addition
            surplus = surplus - addition
    return np.array([reach] + counts)


def uneven_parts(stream_key, amount, total, limit, slope):
    if amount == 2:
        one = jax.random.randint(stream_key, (), max(1, total - limit), min(limit, total - 1) + 1)
        return jnp.stack([one, total - one])
    tallies = jnp.asarray(length_profile(amount, total, limit, slope), jnp.int32)
    couples = (amount - 1) // 2
    donor, sink = tallies[1:1 + 2 * couples:2], tallies[2:2 + 2 * couples:2]
    room = jnp.minimum(donor - 1, limit - sink)
    passed = jax.random.randint(jax.random.fold_in(stream_key, 1), (couples,), 0, 1 << 20) % (room + 1)
    tallies = tallies.at[1:1 + 2 * couples:2].set(donor - passed).at[2:2 + 2 * couples:2].set(sink + passed)
    return tallies[jax.random.permutation(jax.random.fold_in(stream_key, 2), amount)]


def centred(own_key, extent, deviation, bound, cuts=(), kind=jnp.bfloat16):
    array = deviation * jax.random.normal(own_key, extent, jnp.float32)
    if cuts:
        array = array * shard_levels(own_key, extent, cuts, -0.22, 0.18)
    return jnp.clip(array, -bound, bound).astype(kind)


def setup_inputs(seed: int = 0) -> dict:
    key_list = jax.random.split(jax.random.key(seed), 15)
    residual = centred(key_list[0], (PACKS, LENGTH, D), 0.1, 0.59765625, ((0, 8), (1, 16)))
    query_heads = draw_query_heads(jax.random.fold_in(key_list[14], 71), 0)
    key_heads = draw_key_heads(jax.random.fold_in(key_list[14], 71), 0)
    value_heads = centred(key_list[3], (PACKS, LENGTH, H * HD), 1.0, 6.0, ((0, 8), (1, 16)))
    segment_ids = jax.vmap(lambda own: jnp.searchsorted(jnp.cumsum(uneven_parts(own, DOCS, LENGTH, LENGTH // 4, 1)), jnp.arange(LENGTH), side="right"))(jax.random.split(key_list[4], PACKS)).reshape((PACKS, LENGTH)).astype(jnp.int32)
    w_out = centred(key_list[5], (H * HD, D), (H * HD) ** -0.5, 0.125)
    norm_gain = jnp.clip(1.0 + 0.1 * jax.random.normal(key_list[6], (D,), jnp.float32), 0.5, 1.5)
    gate_scores = draw_gate_scores(jax.random.fold_in(key_list[14], 71), 0)
    routes = draw_routes(jax.random.fold_in(key_list[14], 71), 0)
    w_gate = centred(key_list[9], (EXPERTS * 2, D, FF // 2), D ** -0.5, 0.125, ((0, 128),))
    w_up = centred(key_list[10], (EXPERTS * 2, D, FF // 2), D ** -0.5, 0.125, ((0, 128),))
    w_down = centred(key_list[11], (EXPERTS * 2, FF // 2, D), (FF // 4) ** -0.5, 0.3125, ((0, 128),))
    page_holder = draw_page_holder(jax.random.fold_in(key_list[14], 71), 0)
    page_slot = draw_page_slot(jax.random.fold_in(key_list[14], 71), 0)
    return dict(residual=residual, query_heads=query_heads, key_heads=key_heads, value_heads=value_heads, segment_ids=segment_ids, w_out=w_out, norm_gain=norm_gain, gate_scores=gate_scores, routes=routes, w_gate=w_gate, w_up=w_up, w_down=w_down, page_holder=page_holder, page_slot=page_slot)


theta_base = 10000.0
norm_eps = 1e-06
block_limit = 512

def positions_of(segment_row):
    length = segment_row.shape[0]
    indices = jnp.arange(length, dtype=jnp.int32)
    earlier = jnp.concatenate([segment_row[:1] - 1, segment_row[:-1]])
    starts = jnp.where(segment_row != earlier, indices, jnp.zeros_like(indices))
    return indices - lax.cummax(starts, axis=0)

def rotate(values, positions, head_count, head_dim):
    half_dim = head_dim // 2
    freqs = theta_base ** (-jnp.arange(half_dim, dtype=jnp.float32) / half_dim)
    angles = positions.astype(jnp.float32)[:, None] * freqs[None, :]
    cosine = jnp.cos(angles)[:, None, :]
    sine = jnp.sin(angles)[:, None, :]
    shaped = values.astype(jnp.float32).reshape(values.shape[0], head_count, head_dim)
    first_half = shaped[:, :, :half_dim]
    second_half = shaped[:, :, half_dim:]
    turned = jnp.concatenate([first_half * cosine - second_half * sine, second_half * cosine + first_half * sine], axis=-1)
    return turned.reshape(values.shape).astype(jnp.bfloat16)

def attend(query_rot, key_rot, value_rows, segment_row, head_dim):
    length, width = query_rot.shape
    head_count = width // head_dim
    query_split = query_rot.reshape(length, head_count, head_dim)
    key_split = key_rot.reshape(length, head_count, head_dim)
    value_split = value_rows.reshape(length, head_count, head_dim)
    block_rows = min(block_limit, length)
    key_index = jnp.arange(length, dtype=jnp.int32)
    scale = head_dim ** (-0.5)

    def one_block(start):
        query_block = lax.dynamic_slice_in_dim(query_split, start, block_rows, 0)
        query_index = start + jnp.arange(block_rows, dtype=jnp.int32)
        query_segment = lax.dynamic_slice_in_dim(segment_row, start, block_rows, 0)
        scores = jnp.einsum('qhd,khd->hqk', query_block, key_split, preferred_element_type=jnp.float32) * scale
        allowed = (key_index[None, :] <= query_index[:, None]) & (segment_row[None, :] == query_segment[:, None])
        scores = jnp.where(allowed[None, :, :], scores, -jnp.inf)
        highest = lax.optimization_barrier(jnp.max(scores, axis=-1, keepdims=True))
        raised = jnp.exp(scores - highest)
        weights = (raised / lax.optimization_barrier(jnp.sum(raised, axis=-1, keepdims=True))).astype(jnp.bfloat16)
        mixed = jnp.einsum('hqk,khd->qhd', weights, value_split, preferred_element_type=jnp.float32)
        return mixed.astype(jnp.bfloat16).reshape(block_rows, width)
    starts = jnp.arange(length // block_rows, dtype=jnp.int32) * block_rows
    return lax.map(one_block, starts).reshape(length, width)

def gate_weights(scores):
    highest = lax.optimization_barrier(jnp.max(scores, axis=-1, keepdims=True))
    raised = jnp.exp(scores - highest)
    return raised / lax.optimization_barrier(jnp.sum(raised, axis=-1, keepdims=True))

def reference(residual, query_heads, key_heads, value_heads, segment_ids, w_out, norm_gain, gate_scores, routes, w_gate, w_up, w_down, page_holder, page_slot):
    width = H * HD

    def pack_attention(packed):
        query_pack, key_pack, value_pack, segment_row = packed
        positions = positions_of(segment_row)
        query_rot = rotate(query_pack, positions, H, HD)
        key_rot = rotate(key_pack, positions, H, HD)
        return (attend(query_rot, key_rot, value_pack, segment_row, HD), key_rot)
    attended, keys_rot = lax.map(pack_attention, (query_heads, key_heads, value_heads, segment_ids))
    total_rows = PACKS * LENGTH
    hidden = residual.reshape(total_rows, D).astype(jnp.float32) + jnp.dot(attended.reshape(total_rows, width), w_out, preferred_element_type=jnp.float32)
    mean_square = lax.optimization_barrier(jnp.mean(hidden * hidden, axis=-1, keepdims=True))
    normed = (hidden * lax.rsqrt(mean_square + norm_eps) * norm_gain).astype(jnp.bfloat16)
    gates = gate_weights(gate_scores.reshape(total_rows, TOP))
    blocks = total_rows // TOK_DEV
    assigned = routes.reshape(blocks, TOK_DEV * TOP)
    expert_ids = jnp.arange(EXPERTS, dtype=jnp.int32)
    hits = (assigned[:, :, None] == expert_ids).astype(jnp.int32)
    ranks = lax.optimization_barrier(jnp.sum((jnp.cumsum(hits, axis=1) - 1) * hits, axis=-1))
    slot_pos = jnp.arange(blocks, dtype=jnp.int32)[:, None] * CAP + ranks
    token_ids = jnp.arange(total_rows * TOP, dtype=jnp.int32).reshape(blocks, TOK_DEV * TOP) // TOP
    row_table = jnp.full((EXPERTS, blocks * CAP), total_rows, jnp.int32).at[assigned, slot_pos].set(token_ids)
    gate_table = jnp.zeros((EXPERTS, blocks * CAP), jnp.float32).at[assigned, slot_pos].set(gates.reshape(blocks, TOK_DEV * TOP))
    half_ff = FF // 2
    gate_split = w_gate.reshape(EXPERTS, 2, D, half_ff)
    up_split = w_up.reshape(EXPERTS, 2, D, half_ff)
    down_split = w_down.reshape(EXPERTS, 2, half_ff, D)

    def expert_step(running, pieces):
        gate_piece, up_piece, down_piece, row_ids, gate_column = pieces
        chosen = jnp.take(normed, row_ids, axis=0, mode='fill', fill_value=0)
        halves = []
        for half_index in range(2):
            gate_proj = jnp.dot(chosen, gate_piece[half_index], preferred_element_type=jnp.float32)
            up_proj = jnp.dot(chosen, up_piece[half_index], preferred_element_type=jnp.float32)
            activated = (jax.nn.silu(gate_proj) * up_proj).astype(jnp.bfloat16)
            halves.append(jnp.dot(activated, down_piece[half_index], preferred_element_type=jnp.float32).astype(jnp.bfloat16))
        expert_out = (halves[0].astype(jnp.float32) + halves[1].astype(jnp.float32)).astype(jnp.bfloat16)
        running = running.at[row_ids].add(gate_column[:, None] * expert_out.astype(jnp.float32), mode='drop')
        return (running, None)
    moe_sum, _ = lax.scan(expert_step, jnp.zeros((total_rows, D), jnp.float32), (gate_split, up_split, down_split, row_table, gate_table))
    layer_out = (hidden + moe_sum).astype(jnp.bfloat16).reshape(PACKS, LENGTH, D)
    page_data = jnp.concatenate([keys_rot, value_heads], axis=-1).reshape(PACKS, PAGES, PAGE, 2 * width)
    block_of = jnp.broadcast_to(jnp.arange(PAGES, dtype=jnp.int32)[None, :] // PAGES_DEV, (PACKS, PAGES))
    column = page_holder * SLOTS + page_slot
    kv_cache = jnp.zeros((N_SEQ, PACKS * SLOTS, PAGE, 2 * width), jnp.bfloat16).at[block_of, column].set(page_data)
    return (layer_out, kv_cache)
```

```python
import jax
import jax.numpy as jnp
from jax import lax
from jax.sharding import PartitionSpec as P

HD = 128
TOP = 6
PAGE = 16
SEND_CAP = 2


theta_base = 10000.0
norm_eps = 1e-06
block_limit = 512


def positions_of(segment_row):
    length = segment_row.shape[0]
    indices = jnp.arange(length, dtype=jnp.int32)
    earlier = jnp.concatenate([segment_row[:1] - 1, segment_row[:-1]])
    starts = jnp.where(segment_row != earlier, indices, jnp.zeros_like(indices))
    return indices - lax.cummax(starts, axis=0)


def rotate(values, positions, head_count, head_dim):
    half_dim = head_dim // 2
    freqs = theta_base ** (-jnp.arange(half_dim, dtype=jnp.float32) / half_dim)
    angles = positions.astype(jnp.float32)[:, None] * freqs[None, :]
    cosine = jnp.cos(angles)[:, None, :]
    sine = jnp.sin(angles)[:, None, :]
    shaped = values.astype(jnp.float32).reshape(values.shape[0], head_count, head_dim)
    first_half = shaped[:, :, :half_dim]
    second_half = shaped[:, :, half_dim:]
    turned = jnp.concatenate(
        [first_half * cosine - second_half * sine, second_half * cosine + first_half * sine],
        axis=-1,
    )
    return turned.reshape(values.shape).astype(jnp.bfloat16)


def attend(query_rot, key_rot, value_rows, segment_row, head_dim):
    length, width = query_rot.shape
    head_count = width // head_dim
    query_split = query_rot.reshape(length, head_count, head_dim)
    key_split = key_rot.reshape(length, head_count, head_dim)
    value_split = value_rows.reshape(length, head_count, head_dim)
    block_rows = min(block_limit, length)
    key_index = jnp.arange(length, dtype=jnp.int32)
    scale = head_dim ** (-0.5)

    def one_block(start):
        query_block = lax.dynamic_slice_in_dim(query_split, start, block_rows, 0)
        query_index = start + jnp.arange(block_rows, dtype=jnp.int32)
        query_segment = lax.dynamic_slice_in_dim(segment_row, start, block_rows, 0)
        scores = (
            jnp.einsum("qhd,khd->hqk", query_block, key_split, preferred_element_type=jnp.float32)
            * scale
        )
        allowed = (key_index[None, :] <= query_index[:, None]) & (
            segment_row[None, :] == query_segment[:, None]
        )
        scores = jnp.where(allowed[None, :, :], scores, -jnp.inf)
        highest = jnp.max(scores, axis=-1, keepdims=True)
        raised = jnp.exp(scores - highest)
        weights = (raised / jnp.sum(raised, axis=-1, keepdims=True)).astype(jnp.bfloat16)
        mixed = jnp.einsum("hqk,khd->qhd", weights, value_split, preferred_element_type=jnp.float32)
        return mixed.astype(jnp.bfloat16).reshape(block_rows, width)

    starts = jnp.arange(length // block_rows, dtype=jnp.int32) * block_rows
    return lax.map(one_block, starts).reshape(length, width)


def gate_weights(scores):
    highest = jnp.max(scores, axis=-1, keepdims=True)
    raised = jnp.exp(scores - highest)
    return raised / jnp.sum(raised, axis=-1, keepdims=True)


def shards(
    residual,
    query_heads,
    key_heads,
    value_heads,
    segment_ids,
    w_out,
    norm_gain,
    gate_scores,
    routes,
    w_gate,
    w_up,
    w_down,
    page_holder,
    page_slot,
):
    tok_rows = residual.shape[1]
    model_width = residual.shape[2]
    width = query_heads.shape[2]
    head_count = width // HD
    groups = lax.axis_size("seq")
    group_width = width // groups
    seq_index = lax.axis_index("seq")
    exp_index = lax.axis_index("exp")
    swap = [(i, i ^ 1) for i in range(lax.axis_size("exp"))]
    own_half = (w_gate[0], w_up[0], w_down[0])
    halves = (own_half, tuple(lax.ppermute(part, "exp", swap) for part in own_half))
    segment_row = segment_ids[0]
    length = segment_row.shape[0]
    positions = lax.dynamic_slice_in_dim(
        positions_of(segment_row), seq_index * tok_rows, tok_rows, 0
    )
    query_rot = rotate(query_heads[0], positions, head_count, HD)
    key_rot = rotate(key_heads[0], positions, head_count, HD)
    value_own = value_heads[0]
    query_all, key_all, value_all = (
        lax.all_to_all(
            query_rot.reshape(tok_rows, groups, group_width),
            "seq",
            split_axis=1,
            concat_axis=0,
            tiled=True,
        ),
        lax.all_to_all(
            key_rot.reshape(tok_rows, groups, group_width),
            "seq",
            split_axis=1,
            concat_axis=0,
            tiled=True,
        ),
        lax.all_to_all(
            value_own.reshape(tok_rows, groups, group_width),
            "seq",
            split_axis=1,
            concat_axis=0,
            tiled=True,
        ),
    )
    attended = attend(
        query_all.reshape(length, group_width),
        key_all.reshape(length, group_width),
        value_all.reshape(length, group_width),
        segment_row,
        HD,
    )
    regrouped = lax.all_to_all(
        attended.reshape(length, 1, group_width), "seq", split_axis=0, concat_axis=1, tiled=True
    )
    attn_rows = regrouped.reshape(tok_rows, width)
    holders = lax.axis_size("exp")
    page_count = tok_rows // PAGE
    slot_count = holders * SEND_CAP
    page_rows = jnp.concatenate([key_rot, value_own], axis=-1).reshape(page_count, PAGE * 2 * width)
    own_holder = lax.dynamic_slice(
        page_holder, (exp_index, seq_index * page_count), (1, page_count)
    )[0]
    holder_ids = jnp.arange(holders, dtype=jnp.int32)
    own_hits = (own_holder[:, None] == holder_ids[None, :]).astype(jnp.int32)
    own_rank = jnp.sum((jnp.cumsum(own_hits, axis=0) - 1) * own_hits, axis=1)
    target = own_holder * SEND_CAP + own_rank
    selector = (jnp.arange(slot_count, dtype=jnp.int32)[:, None] == target[None, :]).astype(
        jnp.bfloat16
    )
    outgoing = (
        jnp.dot(selector, page_rows, preferred_element_type=jnp.float32)
        .astype(jnp.bfloat16)
        .reshape(holders, SEND_CAP, PAGE * 2 * width)
    )
    incoming = lax.all_to_all(outgoing, "exp", split_axis=0, concat_axis=0, tiled=True)
    source_holder = lax.dynamic_slice_in_dim(page_holder, seq_index * page_count, page_count, 1)
    source_slot = lax.dynamic_slice_in_dim(page_slot, seq_index * page_count, page_count, 1)
    to_self = (source_holder == exp_index).astype(jnp.int32)
    source_rank = jnp.cumsum(to_self, axis=1) - 1
    column = holder_ids[:, None] * SEND_CAP + source_rank
    slot_ids = jnp.arange(slot_count, dtype=jnp.int32)
    slot_hot = ((source_slot[:, :, None] == slot_ids) & (to_self[:, :, None] == 1)).astype(
        jnp.float32
    )
    column_hot = (column[:, :, None] == slot_ids).astype(jnp.float32)
    placement = jnp.einsum("pis,pic->sc", slot_hot, column_hot).astype(jnp.bfloat16)
    kv_block = jnp.dot(
        placement,
        incoming.reshape(slot_count, PAGE * 2 * width),
        preferred_element_type=jnp.float32,
    )
    kv_cache = kv_block.astype(jnp.bfloat16).reshape(1, slot_count, PAGE, 2 * width)
    hidden = residual[0].astype(jnp.float32) + jnp.dot(
        attn_rows, w_out, preferred_element_type=jnp.float32
    )
    mean_square = jnp.mean(hidden * hidden, axis=-1, keepdims=True)
    normed = (hidden * lax.rsqrt(mean_square + norm_eps) * norm_gain).astype(jnp.bfloat16)
    gates = gate_weights(gate_scores[0])
    devices = lax.axis_size(("seq", "exp"))
    experts = devices // 2
    capacity = tok_rows * TOP * 4 // (3 * experts)
    flat_routes = routes[0].reshape(tok_rows * TOP)
    route_hits = (flat_routes[:, None] == jnp.arange(experts, dtype=jnp.int32)[None, :]).astype(
        jnp.int32
    )
    route_rank = jnp.sum((jnp.cumsum(route_hits, axis=0) - 1) * route_hits, axis=1)
    slot_of = flat_routes * capacity + route_rank
    route_slot = (
        slot_of[:, None] == jnp.arange(experts * capacity, dtype=jnp.int32)[None, :]
    ).astype(jnp.bfloat16)
    route_token = (
        (jnp.arange(tok_rows * TOP, dtype=jnp.int32) // TOP)[:, None]
        == jnp.arange(tok_rows, dtype=jnp.int32)[None, :]
    ).astype(jnp.bfloat16)
    dispatch_map = lax.dot_general(
        route_slot, route_token, (((0,), (0,)), ((), ())), preferred_element_type=jnp.float32
    ).astype(jnp.bfloat16)
    packed = jnp.dot(dispatch_map, normed, preferred_element_type=jnp.float32).astype(jnp.bfloat16)
    arrived = lax.all_to_all(
        packed.reshape(devices, capacity // 2, model_width),
        ("seq", "exp"),
        split_axis=0,
        concat_axis=0,
        tiled=True,
    )
    slot_rows = arrived.reshape(devices * capacity // 2, model_width)
    whole_out = None
    for gate_half, up_half, down_half in halves:
        gate_proj = jnp.dot(slot_rows, gate_half, preferred_element_type=jnp.float32)
        up_proj = jnp.dot(slot_rows, up_half, preferred_element_type=jnp.float32)
        activated = (jax.nn.silu(gate_proj) * up_proj).astype(jnp.bfloat16)
        half_out = jnp.dot(activated, down_half, preferred_element_type=jnp.float32)
        whole_out = half_out if whole_out is None else whole_out + half_out
    expert_out = lax.all_to_all(
        whole_out.astype(jnp.bfloat16).reshape(devices, capacity // 2, model_width),
        ("seq", "exp"),
        split_axis=0,
        concat_axis=0,
        tiled=True,
    ).reshape(experts * capacity, model_width)
    per_route = jnp.dot(route_slot, expert_out, preferred_element_type=jnp.float32).reshape(
        tok_rows, TOP, model_width
    )
    moe_sum = jnp.sum(per_route * gates[:, :, None], axis=1)
    layer_out = (hidden + moe_sum).astype(jnp.bfloat16).reshape(1, tok_rows, model_width)
    return (layer_out, kv_cache)


def solution(mesh):
    placed = (
        P("exp", "seq", None),
        P("exp", "seq", None),
        P("exp", "seq", None),
        P("exp", "seq", None),
        P("exp", None),
        P(),
        P(),
        P("exp", "seq", None),
        P("exp", "seq", None),
        P(("seq", "exp"), None, None),
        P(("seq", "exp"), None, None),
        P(("seq", "exp"), None, None),
        P(),
        P(),
    )
    return jax.shard_map(
        shards,
        mesh=mesh,
        in_specs=placed,
        out_specs=(P("exp", "seq", None), P("seq", "exp", None, None)),
        check_vma=False,
    )
```

```python
import jax
import jax.numpy as jnp
from jax import lax
from jax.experimental import pallas as pl
from jax.experimental.pallas import tpu as pltpu
from jax.sharding import PartitionSpec as P

HD = 128
TOP = 6
PAGE = 16
SEND_CAP = 2


theta_base = 10000.0
norm_eps = 1e-06
block_limit = 512


def positions_of(segment_row):
    length = segment_row.shape[0]
    indices = jnp.arange(length, dtype=jnp.int32)
    earlier = jnp.concatenate([segment_row[:1] - 1, segment_row[:-1]])
    starts = jnp.where(segment_row != earlier, indices, jnp.zeros_like(indices))
    return indices - lax.cummax(starts, axis=0)


def rotate(values, positions, head_count, head_dim):
    half_dim = head_dim // 2
    freqs = theta_base ** (-jnp.arange(half_dim, dtype=jnp.float32) / half_dim)
    angles = positions.astype(jnp.float32)[:, None] * freqs[None, :]
    cosine = jnp.cos(angles)[:, None, :]
    sine = jnp.sin(angles)[:, None, :]
    shaped = values.astype(jnp.float32).reshape(values.shape[0], head_count, head_dim)
    first_half = shaped[:, :, :half_dim]
    second_half = shaped[:, :, half_dim:]
    turned = jnp.concatenate(
        [first_half * cosine - second_half * sine, second_half * cosine + first_half * sine],
        axis=-1,
    )
    return turned.reshape(values.shape).astype(jnp.bfloat16)


def attend(query_rot, key_rot, value_rows, segment_row, head_dim):
    length, width = query_rot.shape
    head_count = width // head_dim
    query_split = query_rot.reshape(length, head_count, head_dim)
    key_split = key_rot.reshape(length, head_count, head_dim)
    value_split = value_rows.reshape(length, head_count, head_dim)
    block_rows = min(block_limit, length)
    key_index = jnp.arange(length, dtype=jnp.int32)
    scale = head_dim ** (-0.5)

    def one_block(start):
        query_block = lax.dynamic_slice_in_dim(query_split, start, block_rows, 0)
        query_index = start + jnp.arange(block_rows, dtype=jnp.int32)
        query_segment = lax.dynamic_slice_in_dim(segment_row, start, block_rows, 0)
        scores = (
            jnp.einsum("qhd,khd->hqk", query_block, key_split, preferred_element_type=jnp.float32)
            * scale
        )
        allowed = (key_index[None, :] <= query_index[:, None]) & (
            segment_row[None, :] == query_segment[:, None]
        )
        scores = jnp.where(allowed[None, :, :], scores, -jnp.inf)
        highest = jnp.max(scores, axis=-1, keepdims=True)
        raised = jnp.exp(scores - highest)
        weights = (raised / jnp.sum(raised, axis=-1, keepdims=True)).astype(jnp.bfloat16)
        mixed = jnp.einsum("hqk,khd->qhd", weights, value_split, preferred_element_type=jnp.float32)
        return mixed.astype(jnp.bfloat16).reshape(block_rows, width)

    starts = jnp.arange(length // block_rows, dtype=jnp.int32) * block_rows
    return lax.map(one_block, starts).reshape(length, width)


def gate_weights(scores):
    highest = jnp.max(scores, axis=-1, keepdims=True)
    raised = jnp.exp(scores - highest)
    return raised / jnp.sum(raised, axis=-1, keepdims=True)


SIDE = 4
CHIPS = SIDE**3
GROUP = 16
GROUPS = CHIPS // GROUP
CAP = 16
MESH = pl.DeviceIdType.MESH


def offset_of(i):
    group, along_x, along_y = i // GROUP, (i // SIDE) % SIDE, i % SIDE
    return (group + along_x + along_y) % SIDE, along_x, along_y


def partner(i, backwards):
    seq, exp = lax.axis_index("seq"), lax.axis_index("exp")
    place = (seq // SIDE, seq % SIDE, exp // 2)
    step = offset_of(i)
    z, x, y = [
        (p + SIDE - d) % SIDE if backwards else (p + d) % SIDE for p, d in zip(place, step)
    ]
    return {"seq": z * SIDE + x, "exp": y * 2 + exp % 2}


def slot_experts(slots):
    seq, exp = lax.axis_index("seq"), lax.axis_index("exp")
    i = slots >> 4
    group, along_x, along_y = i >> 4, (i >> 2) & 3, i & 3
    z = (seq // SIDE + group + along_x + along_y) & 3
    x = (seq % SIDE + along_x) & 3
    y = (exp // 2 + along_y) & 3
    return (z * SIDE + x) * SIDE + y


def expert_kernel(
    hidden_ref,
    gain_ref,
    routes_ref,
    scores_ref,
    gate_own,
    up_own,
    down_own,
    gate_other,
    up_other,
    down_other,
    out_ref,
    send,
    recv,
    back,
    ret,
    gate_w,
    up_w,
    down_w,
    mix,
    total,
    weight_sem,
    send_sem,
    back_sem,
    recv_sem,
    ret_sem,
):
    tokens, width = hidden_ref.shape
    rows = GROUP * CAP
    slots = CHIPS * CAP
    barrier = pltpu.get_barrier_semaphore()

    @pl.loop(1, CHIPS)
    def _(i):
        pl.semaphore_signal(
            barrier, inc=1, device_id=partner(i, False), device_id_type=MESH
        )

    loads = []
    for part, (own, other, held) in enumerate(
        ((gate_own, gate_other, gate_w), (up_own, up_other, up_w), (down_own, down_other, down_w))
    ):
        for half, source in enumerate((own, other)):
            copy = pltpu.make_async_copy(source, held.at[half], weight_sem.at[part * 2 + half])
            copy.start()
            loads.append(copy)

    expert_ids = lax.broadcasted_iota(jnp.int32, (tokens, tokens), 0)
    token_ids = lax.broadcasted_iota(jnp.int32, (tokens, tokens), 1)
    scores = scores_ref[...]
    raised = jnp.exp(scores - jnp.max(scores, axis=0, keepdims=True))
    gates = raised / jnp.sum(raised, axis=0, keepdims=True)
    hits = jnp.zeros((tokens, tokens), jnp.float32)
    gate_of = jnp.zeros((tokens, tokens), jnp.float32)
    for k in range(TOP):
        hit = routes_ref[k : k + 1, :] == expert_ids
        hits = hits + jnp.where(hit, 1.0, 0.0)
        gate_of = gate_of + jnp.where(hit, gates[k : k + 1, :], 0.0)
    earlier = jnp.where(expert_ids < token_ids, 1.0, 0.0).astype(jnp.bfloat16)
    rank = jnp.dot(hits.astype(jnp.bfloat16), earlier, preferred_element_type=jnp.float32)
    rank1 = hits * (rank + 1.0)

    hidden = hidden_ref[...]
    mean_square = jnp.mean(hidden * hidden, axis=-1, keepdims=True)
    normed = (hidden * lax.rsqrt(mean_square + norm_eps) * gain_ref[...]).astype(jnp.bfloat16)
    rank1_narrow = rank1.astype(jnp.bfloat16)
    for g in range(GROUPS):
        slot = lax.broadcasted_iota(jnp.int32, (rows, tokens), 0) + g * rows
        expert = lax.broadcasted_iota(jnp.int32, (rows, tokens), 1)
        spread = jnp.where(slot_experts(slot) == expert, 1.0, 0.0).astype(jnp.bfloat16)
        found = jnp.dot(spread, rank1_narrow, preferred_element_type=jnp.float32)
        wanted = ((slot & (CAP - 1)) + 1).astype(jnp.float32)
        pick = jnp.where(found == wanted, 1.0, 0.0).astype(jnp.bfloat16)
        send[pl.ds(g * rows, rows), :] = jnp.dot(
            pick, normed, preferred_element_type=jnp.float32
        ).astype(jnp.bfloat16)

    pl.semaphore_wait(barrier, CHIPS - 1)

    def block(ref, i):
        return ref.at[pl.ds(pl.multiple_of(i * CAP, CAP), CAP)]

    @pl.loop(1, CHIPS)
    def _(i):
        pltpu.make_async_remote_copy(
            src_ref=block(send, i),
            dst_ref=block(recv, i),
            send_sem=send_sem,
            recv_sem=recv_sem.at[i // GROUP],
            device_id=partner(i, False),
            device_id_type=MESH,
        ).start()

    pltpu.make_async_copy(block(send, 0), block(recv, 0), recv_sem.at[0]).start()

    rank1_rows = rank1.T.astype(jnp.bfloat16)
    gate_rows = gate_of.T.astype(jnp.bfloat16)
    for g in range(GROUPS):
        slot = lax.broadcasted_iota(jnp.int32, (tokens, rows), 1) + g * rows
        expert = lax.broadcasted_iota(jnp.int32, (tokens, rows), 0)
        spread = jnp.where(slot_experts(slot) == expert, 1.0, 0.0).astype(jnp.bfloat16)
        found = jnp.dot(rank1_rows, spread, preferred_element_type=jnp.float32)
        taken = jnp.dot(gate_rows, spread, preferred_element_type=jnp.float32)
        wanted = ((slot & (CAP - 1)) + 1).astype(jnp.float32)
        mix[:, g * rows : (g + 1) * rows] = jnp.where(found == wanted, taken, 0.0).astype(
            jnp.bfloat16
        )

    for copy in loads:
        copy.wait()

    across = (((1,), (1,)), ((), ()))

    @pl.loop(0, GROUPS)
    def _(g):
        here = pl.ds(pl.multiple_of(g * rows, rows), rows)
        pltpu.make_async_copy(recv.at[here], recv.at[here], recv_sem.at[g]).wait()
        for half in range(2):
            x = recv[here, :]
            gate = lax.dot_general(x, gate_w[half], across, preferred_element_type=jnp.float32)
            up = lax.dot_general(x, up_w[half], across, preferred_element_type=jnp.float32)
            active = (gate / (1.0 + jnp.exp(-gate)) * up).astype(jnp.bfloat16)
            down = jnp.dot(active, down_w[half], preferred_element_type=jnp.float32)
            if half == 0:
                total[...] = down
            else:
                back[here, :] = (total[...] + down).astype(jnp.bfloat16)

        @pl.loop(0, GROUP)
        def _(j):
            i = g * GROUP + j

            @pl.when(i > 0)
            def _():
                pltpu.make_async_remote_copy(
                    src_ref=block(back, i),
                    dst_ref=block(ret, i),
                    send_sem=back_sem,
                    recv_sem=ret_sem.at[g],
                    device_id=partner(i, True),
                    device_id_type=MESH,
                ).start()

            @pl.when(i == 0)
            def _():
                pltpu.make_async_copy(block(back, 0), block(ret, 0), ret_sem.at[0]).start()

    for g in range(GROUPS):
        here = pl.ds(g * rows, rows)
        pltpu.make_async_copy(ret.at[here], ret.at[here], ret_sem.at[g]).wait()
        part = jnp.dot(
            mix[:, g * rows : (g + 1) * rows], ret[here, :], preferred_element_type=jnp.float32
        )
        before = hidden_ref[...] if g == 0 else total[pl.ds(0, tokens), :]
        if g < GROUPS - 1:
            total[pl.ds(0, tokens), :] = before + part
        else:
            out_ref[...] = (before + part).astype(jnp.bfloat16)
    sent = pl.ds(CAP, slots - CAP)
    pltpu.make_async_copy(send.at[sent], send.at[sent], send_sem).wait()
    pltpu.make_async_copy(back.at[sent], back.at[sent], back_sem).wait()


def run_experts(hidden, norm_gain, scores, routes, own_half, other_half):
    tokens, width = hidden.shape
    half_ff = own_half[2].shape[0]
    slots = CHIPS * CAP
    in_vmem = pl.BlockSpec(memory_space=pltpu.VMEM)
    in_hbm = pl.BlockSpec(memory_space=pl.ANY)
    held = pltpu.VMEM((2, half_ff, width), jnp.bfloat16)
    buffer = pltpu.VMEM((slots, width), jnp.bfloat16)
    return pl.pallas_call(
        expert_kernel,
        out_shape=jax.ShapeDtypeStruct((tokens, width), jnp.bfloat16),
        in_specs=[in_vmem] * 4 + [in_hbm] * 6,
        out_specs=in_vmem,
        scratch_shapes=[
            buffer,
            buffer,
            buffer,
            buffer,
            held,
            held,
            held,
            pltpu.VMEM((tokens, slots), jnp.bfloat16),
            pltpu.VMEM((GROUP * CAP, width), jnp.float32),
            pltpu.SemaphoreType.DMA((6,)),
            pltpu.SemaphoreType.DMA,
            pltpu.SemaphoreType.DMA,
            pltpu.SemaphoreType.DMA((GROUPS,)),
            pltpu.SemaphoreType.DMA((GROUPS,)),
        ],
        compiler_params=pltpu.CompilerParams(
            collective_id=1, has_side_effects=True, vmem_limit_bytes=60 * 1024 * 1024
        ),
        name="experts",
    )(hidden, norm_gain[None, :], routes.T, scores.T, *own_half, *other_half)


def shards(
    residual,
    query_heads,
    key_heads,
    value_heads,
    segment_ids,
    w_out,
    norm_gain,
    gate_scores,
    routes,
    w_gate,
    w_up,
    w_down,
    page_holder,
    page_slot,
):
    tok_rows = residual.shape[1]
    model_width = residual.shape[2]
    width = query_heads.shape[2]
    head_count = width // HD
    groups = lax.axis_size("seq")
    group_width = width // groups
    seq_index = lax.axis_index("seq")
    exp_index = lax.axis_index("exp")
    swap = [(i, i ^ 1) for i in range(lax.axis_size("exp"))]
    own_half = (w_gate[0].T, w_up[0].T, w_down[0])
    other_half = tuple(lax.ppermute(part, "exp", swap) for part in own_half)
    segment_row = segment_ids[0]
    length = segment_row.shape[0]
    positions = lax.dynamic_slice_in_dim(
        positions_of(segment_row), seq_index * tok_rows, tok_rows, 0
    )
    query_rot = rotate(query_heads[0], positions, head_count, HD)
    key_rot = rotate(key_heads[0], positions, head_count, HD)
    value_own = value_heads[0]
    query_all, key_all, value_all = (
        lax.all_to_all(
            query_rot.reshape(tok_rows, groups, group_width),
            "seq",
            split_axis=1,
            concat_axis=0,
            tiled=True,
        ),
        lax.all_to_all(
            key_rot.reshape(tok_rows, groups, group_width),
            "seq",
            split_axis=1,
            concat_axis=0,
            tiled=True,
        ),
        lax.all_to_all(
            value_own.reshape(tok_rows, groups, group_width),
            "seq",
            split_axis=1,
            concat_axis=0,
            tiled=True,
        ),
    )
    attended = attend(
        query_all.reshape(length, group_width),
        key_all.reshape(length, group_width),
        value_all.reshape(length, group_width),
        segment_row,
        HD,
    )
    regrouped = lax.all_to_all(
        attended.reshape(length, 1, group_width), "seq", split_axis=0, concat_axis=1, tiled=True
    )
    attn_rows = regrouped.reshape(tok_rows, width)
    holders = lax.axis_size("exp")
    page_count = tok_rows // PAGE
    slot_count = holders * SEND_CAP
    page_rows = jnp.concatenate([key_rot, value_own], axis=-1).reshape(page_count, PAGE * 2 * width)
    own_holder = lax.dynamic_slice(
        page_holder, (exp_index, seq_index * page_count), (1, page_count)
    )[0]
    holder_ids = jnp.arange(holders, dtype=jnp.int32)
    own_hits = (own_holder[:, None] == holder_ids[None, :]).astype(jnp.int32)
    own_rank = jnp.sum((jnp.cumsum(own_hits, axis=0) - 1) * own_hits, axis=1)
    target = own_holder * SEND_CAP + own_rank
    selector = (jnp.arange(slot_count, dtype=jnp.int32)[:, None] == target[None, :]).astype(
        jnp.bfloat16
    )
    outgoing = (
        jnp.dot(selector, page_rows, preferred_element_type=jnp.float32)
        .astype(jnp.bfloat16)
        .reshape(holders, SEND_CAP, PAGE * 2 * width)
    )
    incoming = lax.all_to_all(outgoing, "exp", split_axis=0, concat_axis=0, tiled=True)
    source_holder = lax.dynamic_slice_in_dim(page_holder, seq_index * page_count, page_count, 1)
    source_slot = lax.dynamic_slice_in_dim(page_slot, seq_index * page_count, page_count, 1)
    to_self = (source_holder == exp_index).astype(jnp.int32)
    source_rank = jnp.cumsum(to_self, axis=1) - 1
    column = holder_ids[:, None] * SEND_CAP + source_rank
    slot_ids = jnp.arange(slot_count, dtype=jnp.int32)
    slot_hot = ((source_slot[:, :, None] == slot_ids) & (to_self[:, :, None] == 1)).astype(
        jnp.float32
    )
    column_hot = (column[:, :, None] == slot_ids).astype(jnp.float32)
    placement = jnp.einsum("pis,pic->sc", slot_hot, column_hot).astype(jnp.bfloat16)
    kv_block = jnp.dot(
        placement,
        incoming.reshape(slot_count, PAGE * 2 * width),
        preferred_element_type=jnp.float32,
    )
    kv_cache = kv_block.astype(jnp.bfloat16).reshape(1, slot_count, PAGE, 2 * width)
    hidden = residual[0].astype(jnp.float32) + jnp.dot(
        attn_rows, w_out, preferred_element_type=jnp.float32
    )
    layer_out = run_experts(
        hidden, norm_gain, gate_scores[0], routes[0], own_half, other_half
    ).reshape(1, tok_rows, model_width)
    return (layer_out, kv_cache)


def solution(mesh):
    placed = (
        P("exp", "seq", None),
        P("exp", "seq", None),
        P("exp", "seq", None),
        P("exp", "seq", None),
        P("exp", None),
        P(),
        P(),
        P("exp", "seq", None),
        P("exp", "seq", None),
        P(("seq", "exp"), None, None),
        P(("seq", "exp"), None, None),
        P(("seq", "exp"), None, None),
        P(),
        P(),
    )
    return jax.shard_map(
        shards,
        mesh=mesh,
        in_specs=placed,
        out_specs=(P("exp", "seq", None), P("seq", "exp", None, None)),
        check_vma=False,
    )
```

```python
import jax
import jax.numpy as jnp
from jax import lax
from jax.experimental import pallas as pl
from jax.experimental.pallas import tpu as pltpu
from jax.sharding import PartitionSpec as P

HD = 128
TOP = 6
PAGE = 16
SEND_CAP = 2


theta_base = 10000.0
norm_eps = 1e-06
Q_ROWS = 256
REACH = 512


SIDE = 4
CHIPS = SIDE**3
GROUP = 16
GROUPS = CHIPS // GROUP
CAP = 16
MESH = pl.DeviceIdType.MESH


def offset_of(i):
    group, along_x, along_y = i // GROUP, (i // SIDE) % SIDE, i % SIDE
    return (group + along_x + along_y) % SIDE, along_x, along_y


def partner(i, backwards):
    seq, exp = lax.axis_index("seq"), lax.axis_index("exp")
    place = (seq // SIDE, seq % SIDE, exp // 2)
    step = offset_of(i)
    z, x, y = [
        (p + SIDE - d) % SIDE if backwards else (p + d) % SIDE for p, d in zip(place, step)
    ]
    return {"seq": z * SIDE + x, "exp": y * 2 + exp % 2}


def slot_experts(slots):
    seq, exp = lax.axis_index("seq"), lax.axis_index("exp")
    i = slots >> 4
    group, along_x, along_y = i >> 4, (i >> 2) & 3, i & 3
    z = (seq // SIDE + group + along_x + along_y) & 3
    x = (seq % SIDE + along_x) & 3
    y = (exp // 2 + along_y) & 3
    return (z * SIDE + x) * SIDE + y


def expert_kernel(
    hidden_ref,
    gain_ref,
    routes_ref,
    scores_ref,
    gate_own,
    up_own,
    down_own,
    gate_other,
    up_other,
    down_other,
    out_ref,
    send,
    recv,
    back,
    ret,
    gate_w,
    up_w,
    down_w,
    mix,
    total,
    weight_sem,
    send_sem,
    back_sem,
    recv_sem,
    ret_sem,
):
    tokens, width = hidden_ref.shape
    rows = GROUP * CAP
    slots = CHIPS * CAP
    barrier = pltpu.get_barrier_semaphore()

    @pl.loop(1, CHIPS)
    def _(i):
        pl.semaphore_signal(
            barrier, inc=1, device_id=partner(i, False), device_id_type=MESH
        )

    loads = []
    for part, (own, other, held) in enumerate(
        ((gate_own, gate_other, gate_w), (up_own, up_other, up_w), (down_own, down_other, down_w))
    ):
        for half, source in enumerate((own, other)):
            copy = pltpu.make_async_copy(source, held.at[half], weight_sem.at[part * 2 + half])
            copy.start()
            loads.append(copy)

    expert_ids = lax.broadcasted_iota(jnp.int32, (tokens, tokens), 0)
    token_ids = lax.broadcasted_iota(jnp.int32, (tokens, tokens), 1)
    scores = scores_ref[...]
    raised = jnp.exp(scores - jnp.max(scores, axis=0, keepdims=True))
    gates = raised / jnp.sum(raised, axis=0, keepdims=True)
    hits = jnp.zeros((tokens, tokens), jnp.float32)
    gate_of = jnp.zeros((tokens, tokens), jnp.float32)
    for k in range(TOP):
        hit = routes_ref[k : k + 1, :] == expert_ids
        hits = hits + jnp.where(hit, 1.0, 0.0)
        gate_of = gate_of + jnp.where(hit, gates[k : k + 1, :], 0.0)
    earlier = jnp.where(expert_ids < token_ids, 1.0, 0.0).astype(jnp.bfloat16)
    rank = jnp.dot(hits.astype(jnp.bfloat16), earlier, preferred_element_type=jnp.float32)
    rank1 = hits * (rank + 1.0)

    hidden = hidden_ref[...]
    mean_square = jnp.mean(hidden * hidden, axis=-1, keepdims=True)
    normed = (hidden * lax.rsqrt(mean_square + norm_eps) * gain_ref[...]).astype(jnp.bfloat16)
    rank1_narrow = rank1.astype(jnp.bfloat16)
    for g in range(GROUPS):
        slot = lax.broadcasted_iota(jnp.int32, (rows, tokens), 0) + g * rows
        expert = lax.broadcasted_iota(jnp.int32, (rows, tokens), 1)
        spread = jnp.where(slot_experts(slot) == expert, 1.0, 0.0).astype(jnp.bfloat16)
        found = jnp.dot(spread, rank1_narrow, preferred_element_type=jnp.float32)
        wanted = ((slot & (CAP - 1)) + 1).astype(jnp.float32)
        pick = jnp.where(found == wanted, 1.0, 0.0).astype(jnp.bfloat16)
        send[pl.ds(g * rows, rows), :] = jnp.dot(
            pick, normed, preferred_element_type=jnp.float32
        ).astype(jnp.bfloat16)

    pl.semaphore_wait(barrier, CHIPS - 1)

    def block(ref, i):
        return ref.at[pl.ds(pl.multiple_of(i * CAP, CAP), CAP)]

    @pl.loop(1, CHIPS)
    def _(i):
        pltpu.make_async_remote_copy(
            src_ref=block(send, i),
            dst_ref=block(recv, i),
            send_sem=send_sem,
            recv_sem=recv_sem.at[i // GROUP],
            device_id=partner(i, False),
            device_id_type=MESH,
        ).start()

    pltpu.make_async_copy(block(send, 0), block(recv, 0), recv_sem.at[0]).start()

    rank1_rows = rank1.T.astype(jnp.bfloat16)
    gate_rows = gate_of.T.astype(jnp.bfloat16)
    for g in range(GROUPS):
        slot = lax.broadcasted_iota(jnp.int32, (tokens, rows), 1) + g * rows
        expert = lax.broadcasted_iota(jnp.int32, (tokens, rows), 0)
        spread = jnp.where(slot_experts(slot) == expert, 1.0, 0.0).astype(jnp.bfloat16)
        found = jnp.dot(rank1_rows, spread, preferred_element_type=jnp.float32)
        taken = jnp.dot(gate_rows, spread, preferred_element_type=jnp.float32)
        wanted = ((slot & (CAP - 1)) + 1).astype(jnp.float32)
        mix[:, g * rows : (g + 1) * rows] = jnp.where(found == wanted, taken, 0.0).astype(
            jnp.bfloat16
        )

    for copy in loads:
        copy.wait()

    across = (((1,), (1,)), ((), ()))

    @pl.loop(0, GROUPS)
    def _(g):
        here = pl.ds(pl.multiple_of(g * rows, rows), rows)
        pltpu.make_async_copy(recv.at[here], recv.at[here], recv_sem.at[g]).wait()
        for half in range(2):
            x = recv[here, :]
            gate = lax.dot_general(x, gate_w[half], across, preferred_element_type=jnp.float32)
            up = lax.dot_general(x, up_w[half], across, preferred_element_type=jnp.float32)
            active = (gate / (1.0 + jnp.exp(-gate)) * up).astype(jnp.bfloat16)
            down = jnp.dot(active, down_w[half], preferred_element_type=jnp.float32)
            if half == 0:
                total[...] = down
            else:
                back[here, :] = (total[...] + down).astype(jnp.bfloat16)

        @pl.loop(0, GROUP)
        def _(j):
            i = g * GROUP + j

            @pl.when(i > 0)
            def _():
                pltpu.make_async_remote_copy(
                    src_ref=block(back, i),
                    dst_ref=block(ret, i),
                    send_sem=back_sem,
                    recv_sem=ret_sem.at[g],
                    device_id=partner(i, True),
                    device_id_type=MESH,
                ).start()

            @pl.when(i == 0)
            def _():
                pltpu.make_async_copy(block(back, 0), block(ret, 0), ret_sem.at[0]).start()

    for g in range(GROUPS):
        here = pl.ds(g * rows, rows)
        pltpu.make_async_copy(ret.at[here], ret.at[here], ret_sem.at[g]).wait()
        part = jnp.dot(
            mix[:, g * rows : (g + 1) * rows], ret[here, :], preferred_element_type=jnp.float32
        )
        before = hidden_ref[...] if g == 0 else total[pl.ds(0, tokens), :]
        if g < GROUPS - 1:
            total[pl.ds(0, tokens), :] = before + part
        else:
            out_ref[...] = (before + part).astype(jnp.bfloat16)
    sent = pl.ds(CAP, slots - CAP)
    pltpu.make_async_copy(send.at[sent], send.at[sent], send_sem).wait()
    pltpu.make_async_copy(back.at[sent], back.at[sent], back_sem).wait()


def run_experts(hidden, norm_gain, scores, routes, own_half, other_half):
    tokens, width = hidden.shape
    half_ff = own_half[2].shape[0]
    slots = CHIPS * CAP
    in_vmem = pl.BlockSpec(memory_space=pltpu.VMEM)
    in_hbm = pl.BlockSpec(memory_space=pl.ANY)
    held = pltpu.VMEM((2, half_ff, width), jnp.bfloat16)
    buffer = pltpu.VMEM((slots, width), jnp.bfloat16)
    return pl.pallas_call(
        expert_kernel,
        out_shape=jax.ShapeDtypeStruct((tokens, width), jnp.bfloat16),
        in_specs=[in_vmem] * 4 + [in_hbm] * 6,
        out_specs=in_vmem,
        scratch_shapes=[
            buffer,
            buffer,
            buffer,
            buffer,
            held,
            held,
            held,
            pltpu.VMEM((tokens, slots), jnp.bfloat16),
            pltpu.VMEM((GROUP * CAP, width), jnp.float32),
            pltpu.SemaphoreType.DMA((6,)),
            pltpu.SemaphoreType.DMA,
            pltpu.SemaphoreType.DMA,
            pltpu.SemaphoreType.DMA((GROUPS,)),
            pltpu.SemaphoreType.DMA((GROUPS,)),
        ],
        compiler_params=pltpu.CompilerParams(
            collective_id=1, has_side_effects=True, vmem_limit_bytes=60 * 1024 * 1024
        ),
        name="experts",
    )(hidden, norm_gain[None, :], routes.T, scores.T, *own_half, *other_half)


def front_kernel(
    query_ref,
    key_ref,
    value_ref,
    residual_ref,
    cosine_ref,
    sine_ref,
    segment_ref,
    select_ref,
    w_out_hbm,
    hidden_ref,
    pages_in,
    send,
    recv,
    page_rows,
    pages_out,
    mixed,
    attn_rows,
    w_out,
    weight_sem,
    send_sem,
    recv_sem,
    page_send_sem,
    page_recv_sem,
    back_sem,
    ret_sem,
):
    tokens, width = query_ref.shape
    length = recv.shape[0]
    heads = width // HD
    peers = length // tokens
    holders = lax.axis_size("exp")
    page_block = pages_out.shape[0] // holders
    seq, exp = lax.axis_index("seq"), lax.axis_index("exp")
    barrier = pltpu.get_barrier_semaphore()

    def seq_peer(i):
        return ((seq // SIDE + i // SIDE) % SIDE) * SIDE + (seq % SIDE + i % SIDE) % SIDE

    @pl.loop(1, peers)
    def _(i):
        pl.semaphore_signal(barrier, inc=1, device_id={"seq": seq_peer(i)}, device_id_type=MESH)

    @pl.loop(1, holders)
    def _(i):
        pl.semaphore_signal(
            barrier, inc=1, device_id={"exp": (exp + i) % holders}, device_id_type=MESH
        )

    load = pltpu.make_async_copy(w_out_hbm, w_out, weight_sem)
    load.start()

    def rotated(ref, cols):
        u = ref[:, cols].astype(jnp.float32)
        turned = pltpu.roll(u, HD // 2, 1)
        return (u * cosine_ref[...] + turned * sine_ref[...]).astype(jnp.bfloat16)

    @pl.loop(0, heads)
    def _(h):
        cols = pl.ds(pl.multiple_of(h * HD, HD), HD)
        value_cols = pl.ds(pl.multiple_of(width + h * HD, HD), HD)
        key_rot = rotated(key_ref, cols)
        value = value_ref[:, cols]
        send[h, :, 0:HD] = rotated(query_ref, cols)
        send[h, :, HD : 2 * HD] = key_rot
        send[h, :, 2 * HD : 3 * HD] = value
        page_rows[:, cols] = key_rot
        page_rows[:, value_cols] = value

    pl.semaphore_wait(barrier, peers - 1 + holders - 1)

    own_rows = pl.ds(pl.multiple_of(seq * tokens, tokens), tokens)
    own_cols = pl.ds(pl.multiple_of(seq * HD, HD), HD)

    @pl.loop(1, peers)
    def _(i):
        j = seq_peer(i)
        pltpu.make_async_remote_copy(
            src_ref=send.at[j],
            dst_ref=recv.at[own_rows],
            send_sem=send_sem,
            recv_sem=recv_sem,
            device_id={"seq": j},
            device_id_type=MESH,
        ).start()

    pltpu.make_async_copy(send.at[seq], recv.at[own_rows], recv_sem).start()

    @pl.loop(0, 2 * width // 512)
    def _(n):
        cols = pl.ds(pl.multiple_of(n * 512, 512), 512)
        pages_out[:, cols] = jnp.dot(
            select_ref[...], page_rows[:, cols], preferred_element_type=jnp.float32
        ).astype(jnp.bfloat16)

    def page_slice(ref, holder):
        return ref.at[pl.ds(pl.multiple_of(holder * page_block, page_block), page_block)]

    @pl.loop(1, holders)
    def _(i):
        to = (exp + i) % holders
        pltpu.make_async_remote_copy(
            src_ref=page_slice(pages_out, to),
            dst_ref=page_slice(pages_in, exp),
            send_sem=page_send_sem,
            recv_sem=page_recv_sem,
            device_id={"exp": to},
            device_id_type=MESH,
        ).start()

    pltpu.make_async_copy(
        page_slice(pages_out, exp), page_slice(pages_in, exp), page_recv_sem
    ).start()

    pltpu.make_async_copy(recv, recv, recv_sem).wait()

    blocks = length // Q_ROWS
    window = Q_ROWS + REACH

    @pl.loop(0, blocks)
    def _(i):
        start = pl.multiple_of(((i + seq // 2) % blocks) * Q_ROWS, Q_ROWS)
        first = pl.multiple_of(jnp.maximum(start - REACH, 0), Q_ROWS)
        here = pl.ds(start, Q_ROWS)
        keys = pl.ds(first, window)
        scores = lax.dot_general(
            recv[here, 0:HD],
            recv[keys, HD : 2 * HD],
            (((1,), (1,)), ((), ())),
            preferred_element_type=jnp.float32,
        ) * (HD**-0.5)
        query_segment = jnp.broadcast_to(segment_ref[:, here], (HD, Q_ROWS)).T[:, 0:1]
        query_index = start + lax.broadcasted_iota(jnp.int32, (Q_ROWS, window), 0)
        key_index = first + lax.broadcasted_iota(jnp.int32, (Q_ROWS, window), 1)
        allowed = (key_index <= query_index) & (segment_ref[:, keys] == query_segment)
        scores = jnp.where(allowed, scores, -1e30)
        raised = jnp.exp(scores - jnp.max(scores, axis=-1, keepdims=True))
        weights = (raised * (1.0 / jnp.sum(raised, axis=-1, keepdims=True))).astype(jnp.bfloat16)
        mixed[here, :] = jnp.dot(
            weights, recv[keys, 2 * HD : 3 * HD], preferred_element_type=jnp.float32
        ).astype(jnp.bfloat16)
        for part in range(Q_ROWS // tokens):
            j = start // tokens + part
            rows = pl.ds(pl.multiple_of(j * tokens, tokens), tokens)

            @pl.when(j != seq)
            def _():
                pltpu.make_async_remote_copy(
                    src_ref=mixed.at[rows],
                    dst_ref=attn_rows.at[:, own_cols],
                    send_sem=back_sem,
                    recv_sem=ret_sem,
                    device_id={"seq": j},
                    device_id_type=MESH,
                ).start()

            @pl.when(j == seq)
            def _():
                pltpu.make_async_copy(mixed.at[rows], attn_rows.at[:, own_cols], ret_sem).start()

    load.wait()
    pltpu.make_async_copy(attn_rows, attn_rows, ret_sem).wait()

    @pl.loop(0, width // 512)
    def _(n):
        cols = pl.ds(pl.multiple_of(n * 512, 512), 512)
        hidden_ref[:, cols] = residual_ref[:, cols].astype(jnp.float32) + jnp.dot(
            attn_rows[...], w_out[:, cols], preferred_element_type=jnp.float32
        )

    pltpu.make_async_copy(pages_in, pages_in, page_recv_sem).wait()
    sent = send.at[pl.ds(0, peers - 1)]
    pltpu.make_async_copy(sent, sent, send_sem).wait()
    sent_back = mixed.at[pl.ds(0, length - tokens)]
    pltpu.make_async_copy(sent_back, sent_back, back_sem).wait()
    sent_pages = pages_out.at[pl.ds(0, page_block * (holders - 1))]
    pltpu.make_async_copy(sent_pages, sent_pages, page_send_sem).wait()


def run_front(query, key, value, residual, cosine, sine, segment_row, select, w_out):
    tokens, width = query.shape
    length = segment_row.shape[0]
    heads = width // HD
    page_rows = select.shape[0]
    in_vmem = pl.BlockSpec(memory_space=pltpu.VMEM)
    in_hbm = pl.BlockSpec(memory_space=pl.ANY)
    return pl.pallas_call(
        front_kernel,
        out_shape=(
            jax.ShapeDtypeStruct((tokens, width), jnp.float32),
            jax.ShapeDtypeStruct((page_rows, 2 * width), jnp.bfloat16),
        ),
        in_specs=[in_vmem] * 8 + [in_hbm],
        out_specs=(in_vmem, in_hbm),
        scratch_shapes=[
            pltpu.VMEM((heads, tokens, 3 * HD), jnp.bfloat16),
            pltpu.VMEM((length, 3 * HD), jnp.bfloat16),
            pltpu.VMEM((tokens, 2 * width), jnp.bfloat16),
            pltpu.VMEM((page_rows, 2 * width), jnp.bfloat16),
            pltpu.VMEM((length, HD), jnp.bfloat16),
            pltpu.VMEM((tokens, width), jnp.bfloat16),
            pltpu.VMEM(w_out.shape, jnp.bfloat16),
        ]
        + [pltpu.SemaphoreType.DMA] * 7,
        compiler_params=pltpu.CompilerParams(
            collective_id=2, has_side_effects=True, vmem_limit_bytes=40 * 1024 * 1024
        ),
        name="front",
    )(
        query,
        key,
        value,
        residual,
        cosine,
        sine,
        segment_row.astype(jnp.float32)[None, :],
        select,
        w_out,
    )


def rotation_tables(segment_row, start, count):
    length = segment_row.shape[0]
    index = jnp.arange(length, dtype=jnp.int32)
    own = lax.dynamic_slice_in_dim(segment_row, start, count, 0)
    own_index = start + jnp.arange(count, dtype=jnp.int32)
    before = (segment_row[None, :] == own[:, None]) & (index[None, :] < own_index[:, None])
    positions = jnp.sum(before.astype(jnp.int32), axis=1)
    half = HD // 2
    lane = jnp.arange(HD, dtype=jnp.int32)
    freqs = theta_base ** (-(lane % half).astype(jnp.float32) / half)
    angles = positions.astype(jnp.float32)[:, None] * freqs[None, :]
    sign = jnp.where(lane < half, -1.0, 1.0)
    return jnp.cos(angles), jnp.sin(angles) * sign


def token_level(hot):
    slots, pages = hot.shape
    row = jnp.arange(PAGE, dtype=jnp.int32)
    wide = hot[:, None, :, None] & (row[:, None] == row[None, :])[None, :, None, :]
    return wide.reshape(slots * PAGE, pages * PAGE).astype(jnp.bfloat16)


def shards(
    residual,
    query_heads,
    key_heads,
    value_heads,
    segment_ids,
    w_out,
    norm_gain,
    gate_scores,
    routes,
    w_gate,
    w_up,
    w_down,
    page_holder,
    page_slot,
):
    tok_rows = residual.shape[1]
    model_width = residual.shape[2]
    width = query_heads.shape[2]
    seq_index = lax.axis_index("seq")
    exp_index = lax.axis_index("exp")
    holders = lax.axis_size("exp")
    swap = [(i, i ^ 1) for i in range(holders)]
    own_half = (w_gate[0].T, w_up[0].T, w_down[0])
    other_half = tuple(lax.ppermute(part, "exp", swap) for part in own_half)
    segment_row = segment_ids[0]
    cosine, sine = rotation_tables(segment_row, seq_index * tok_rows, tok_rows)

    page_count = tok_rows // PAGE
    slot_count = holders * SEND_CAP
    own_holder = lax.dynamic_slice(
        page_holder, (exp_index, seq_index * page_count), (1, page_count)
    )[0]
    page = jnp.arange(page_count, dtype=jnp.int32)
    earlier = page[None, :] < page[:, None]
    own_rank = jnp.sum(
        ((own_holder[None, :] == own_holder[:, None]) & earlier).astype(jnp.int32), axis=1
    )
    target = own_holder * SEND_CAP + own_rank
    slot_ids = jnp.arange(slot_count, dtype=jnp.int32)
    select = token_level(slot_ids[:, None] == target[None, :])

    hidden, incoming = run_front(
        query_heads[0],
        key_heads[0],
        value_heads[0],
        residual[0],
        cosine,
        sine,
        segment_row,
        select,
        w_out,
    )

    source_holder = lax.dynamic_slice_in_dim(page_holder, seq_index * page_count, page_count, 1)
    source_slot = lax.dynamic_slice_in_dim(page_slot, seq_index * page_count, page_count, 1)
    to_self = source_holder == exp_index
    source_rank = jnp.sum((to_self[:, None, :] & earlier[None]).astype(jnp.int32), axis=2)
    ranks = jnp.arange(SEND_CAP, dtype=jnp.int32)
    taken = to_self[:, None, :] & (source_rank[:, None, :] == ranks[None, :, None])
    slot_of = jnp.sum(jnp.where(taken, source_slot[:, None, :] + 1, 0), axis=2) - 1
    placement = token_level(slot_ids[:, None] == slot_of.reshape(slot_count)[None, :])
    kv_block = jnp.dot(placement, incoming, preferred_element_type=jnp.float32)
    kv_cache = kv_block.astype(jnp.bfloat16).reshape(1, slot_count, PAGE, 2 * width)
    layer_out = run_experts(
        hidden, norm_gain, gate_scores[0], routes[0], own_half, other_half
    ).reshape(1, tok_rows, model_width)
    return (layer_out, kv_cache)


def solution(mesh):
    placed = (
        P("exp", "seq", None),
        P("exp", "seq", None),
        P("exp", "seq", None),
        P("exp", "seq", None),
        P("exp", None),
        P(),
        P(),
        P("exp", "seq", None),
        P("exp", "seq", None),
        P(("seq", "exp"), None, None),
        P(("seq", "exp"), None, None),
        P(("seq", "exp"), None, None),
        P(),
        P(),
    )
    return jax.shard_map(
        shards,
        mesh=mesh,
        in_specs=placed,
        out_specs=(P("exp", "seq", None), P("seq", "exp", None, None)),
        check_vma=False,
    )
```

```python
import math

import jax
import jax.numpy as jnp
from jax import lax
from jax.experimental import pallas as pl
from jax.experimental.pallas import tpu as pltpu
from jax.sharding import PartitionSpec as P

HD = 128
TOP = 6
PAGE = 16
SEND_CAP = 2


theta_base = 10000.0
norm_eps = 1e-06
Q_ROWS = 256
REACH = 512


SIDE = 4
CHIPS = SIDE**3
GROUP = 16
GROUPS = CHIPS // GROUP
CAP = 16
MESH = pl.DeviceIdType.MESH


def offset_of(i):
    group, along_x, along_y = i // GROUP, (i // SIDE) % SIDE, i % SIDE
    return (group + along_x + along_y) % SIDE, along_x, along_y


def partner(i, backwards):
    seq, exp = lax.axis_index("seq"), lax.axis_index("exp")
    place = (seq // SIDE, seq % SIDE, exp // 2)
    step = offset_of(i)
    z, x, y = [
        (p + SIDE - d) % SIDE if backwards else (p + d) % SIDE for p, d in zip(place, step)
    ]
    return {"seq": z * SIDE + x, "exp": y * 2 + exp % 2}


def slot_experts(slots):
    seq, exp = lax.axis_index("seq"), lax.axis_index("exp")
    i = slots >> 4
    group, along_x, along_y = i >> 4, (i >> 2) & 3, i & 3
    z = (seq // SIDE + group + along_x + along_y) & 3
    x = (seq % SIDE + along_x) & 3
    y = (exp // 2 + along_y) & 3
    return (z * SIDE + x) * SIDE + y


def expert_kernel(
    hidden_ref,
    gain_ref,
    routes_ref,
    scores_ref,
    gate_own,
    up_own,
    down_own,
    gate_other,
    up_other,
    down_other,
    out_ref,
    send,
    recv,
    back,
    ret,
    gate_w,
    up_w,
    down_w,
    mix,
    total,
    weight_sem,
    send_sem,
    back_sem,
    recv_sem,
    ret_sem,
):
    tokens, width = hidden_ref.shape
    rows = GROUP * CAP
    slots = CHIPS * CAP
    barrier = pltpu.get_barrier_semaphore()

    @pl.loop(1, CHIPS)
    def _(i):
        pl.semaphore_signal(
            barrier, inc=1, device_id=partner(i, False), device_id_type=MESH
        )

    loads = []
    for part, (own, other, held) in enumerate(
        ((gate_own, gate_other, gate_w), (up_own, up_other, up_w), (down_own, down_other, down_w))
    ):
        for half, source in enumerate((own, other)):
            copy = pltpu.make_async_copy(source, held.at[half], weight_sem.at[part * 2 + half])
            copy.start()
            loads.append(copy)

    expert_ids = lax.broadcasted_iota(jnp.int32, (tokens, tokens), 0)
    token_ids = lax.broadcasted_iota(jnp.int32, (tokens, tokens), 1)
    scores = scores_ref[...]
    raised = jnp.exp(scores - jnp.max(scores, axis=0, keepdims=True))
    gates = raised / jnp.sum(raised, axis=0, keepdims=True)
    hits = jnp.zeros((tokens, tokens), jnp.float32)
    gate_of = jnp.zeros((tokens, tokens), jnp.float32)
    for k in range(TOP):
        hit = routes_ref[k] == expert_ids
        hits = hits + jnp.where(hit, 1.0, 0.0)
        gate_of = gate_of + jnp.where(hit, gates[k], 0.0)
    earlier = jnp.where(expert_ids < token_ids, 1.0, 0.0).astype(jnp.bfloat16)
    rank = jnp.dot(hits.astype(jnp.bfloat16), earlier, preferred_element_type=jnp.float32)
    rank1 = hits * (rank + 1.0)

    hidden = hidden_ref[...]
    mean_square = jnp.mean(hidden * hidden, axis=-1, keepdims=True)
    normed = (hidden * lax.rsqrt(mean_square + norm_eps) * gain_ref[...]).astype(jnp.bfloat16)
    rank1_narrow = rank1.astype(jnp.bfloat16)

    def block(ref, i):
        return ref.at[pl.ds(pl.multiple_of(i * CAP, CAP), CAP)]

    def build(g):
        slot = lax.broadcasted_iota(jnp.int32, (rows, tokens), 0) + g * rows
        expert = lax.broadcasted_iota(jnp.int32, (rows, tokens), 1)
        spread = jnp.where(slot_experts(slot) == expert, 1.0, 0.0).astype(jnp.bfloat16)
        found = jnp.dot(spread, rank1_narrow, preferred_element_type=jnp.float32)
        wanted = ((slot & (CAP - 1)) + 1).astype(jnp.float32)
        pick = jnp.where(found == wanted, 1.0, 0.0).astype(jnp.bfloat16)
        send[pl.ds(g * rows, rows), :] = jnp.dot(
            pick, normed, preferred_element_type=jnp.float32
        ).astype(jnp.bfloat16)

    def dispatch(g):
        @pl.loop(max(g * GROUP, 1), (g + 1) * GROUP)
        def _(i):
            pltpu.make_async_remote_copy(
                src_ref=block(send, i),
                dst_ref=block(recv, i),
                send_sem=send_sem,
                recv_sem=recv_sem.at[g],
                device_id=partner(i, False),
                device_id_type=MESH,
            ).start()

    build(0)
    pl.semaphore_wait(barrier, CHIPS - 1)
    dispatch(0)
    pltpu.make_async_copy(block(send, 0), block(recv, 0), recv_sem.at[0]).start()
    for g in range(1, GROUPS):
        build(g)
        if g > 1:
            dispatch(g - 1)

    rank1_rows = rank1.T.astype(jnp.bfloat16)
    gate_rows = gate_of.T.astype(jnp.bfloat16)
    for g in range(GROUPS):
        slot = lax.broadcasted_iota(jnp.int32, (tokens, rows), 1) + g * rows
        expert = lax.broadcasted_iota(jnp.int32, (tokens, rows), 0)
        spread = jnp.where(slot_experts(slot) == expert, 1.0, 0.0).astype(jnp.bfloat16)
        found = jnp.dot(rank1_rows, spread, preferred_element_type=jnp.float32)
        taken = jnp.dot(gate_rows, spread, preferred_element_type=jnp.float32)
        wanted = ((slot & (CAP - 1)) + 1).astype(jnp.float32)
        mix[:, g * rows : (g + 1) * rows] = jnp.where(found == wanted, taken, 0.0).astype(
            jnp.bfloat16
        )
        if g == 0:
            dispatch(GROUPS - 1)

    for copy in loads:
        copy.wait()

    across = (((1,), (1,)), ((), ()))

    @pl.loop(0, GROUPS)
    def _(g):
        here = pl.ds(pl.multiple_of(g * rows, rows), rows)
        pltpu.make_async_copy(recv.at[here], recv.at[here], recv_sem.at[g]).wait()
        for half in range(2):
            x = recv[here, :]
            gate = lax.dot_general(x, gate_w[half], across, preferred_element_type=jnp.float32)
            up = lax.dot_general(x, up_w[half], across, preferred_element_type=jnp.float32)
            active = (gate / (1.0 + jnp.exp(-gate)) * up).astype(jnp.bfloat16)
            down = jnp.dot(active, down_w[half], preferred_element_type=jnp.float32)
            if half == 0:
                total[...] = down
            else:
                back[here, :] = (total[...] + down).astype(jnp.bfloat16)

        @pl.loop(0, GROUP)
        def _(j):
            i = g * GROUP + j

            @pl.when(i > 0)
            def _():
                pltpu.make_async_remote_copy(
                    src_ref=block(back, i),
                    dst_ref=block(ret, i),
                    send_sem=back_sem,
                    recv_sem=ret_sem.at[g],
                    device_id=partner(i, True),
                    device_id_type=MESH,
                ).start()

            @pl.when(i == 0)
            def _():
                pltpu.make_async_copy(block(back, 0), block(ret, 0), ret_sem.at[0]).start()

    for g in range(GROUPS):
        here = pl.ds(g * rows, rows)
        pltpu.make_async_copy(ret.at[here], ret.at[here], ret_sem.at[g]).wait()
        part = jnp.dot(
            mix[:, g * rows : (g + 1) * rows], ret[here, :], preferred_element_type=jnp.float32
        )
        before = hidden_ref[...] if g == 0 else total[pl.ds(0, tokens), :]
        if g < GROUPS - 1:
            total[pl.ds(0, tokens), :] = before + part
        else:
            out_ref[...] = (before + part).astype(jnp.bfloat16)
    sent = pl.ds(CAP, slots - CAP)
    pltpu.make_async_copy(send.at[sent], send.at[sent], send_sem).wait()
    pltpu.make_async_copy(back.at[sent], back.at[sent], back_sem).wait()


def run_experts(hidden, norm_gain, scores, routes, own_half, other_half):
    tokens, width = hidden.shape
    half_ff = own_half[2].shape[0]
    slots = CHIPS * CAP
    in_vmem = pl.BlockSpec(memory_space=pltpu.VMEM)
    in_hbm = pl.BlockSpec(memory_space=pl.ANY)
    held = pltpu.VMEM((2, half_ff, width), jnp.bfloat16)
    buffer = pltpu.VMEM((slots, width), jnp.bfloat16)
    return pl.pallas_call(
        expert_kernel,
        out_shape=jax.ShapeDtypeStruct((tokens, width), jnp.bfloat16),
        in_specs=[in_vmem] * 4 + [in_hbm] * 6,
        out_specs=in_vmem,
        scratch_shapes=[
            buffer,
            buffer,
            buffer,
            buffer,
            held,
            held,
            held,
            pltpu.VMEM((tokens, slots), jnp.bfloat16),
            pltpu.VMEM((GROUP * CAP, width), jnp.float32),
            pltpu.SemaphoreType.DMA((6,)),
            pltpu.SemaphoreType.DMA,
            pltpu.SemaphoreType.DMA,
            pltpu.SemaphoreType.DMA((GROUPS,)),
            pltpu.SemaphoreType.DMA((GROUPS,)),
        ],
        compiler_params=pltpu.CompilerParams(
            collective_id=1, has_side_effects=True, vmem_limit_bytes=60 * 1024 * 1024
        ),
        name="experts",
    )(
        hidden,
        norm_gain[None, :],
        jnp.transpose(routes, (2, 0, 1)),
        jnp.transpose(scores, (2, 0, 1)),
        *own_half,
        *other_half,
    )


def front_kernel(
    query_ref,
    key_ref,
    value_ref,
    residual_ref,
    segment_ids_ref,
    holder_ref,
    slot_ref,
    w_out_hbm,
    hidden_ref,
    placement_ref,
    pages_in,
    send,
    recv,
    page_rows,
    pages_out,
    mixed,
    attn_rows,
    w_out,
    segment_ref,
    cosine_ref,
    sine_ref,
    weight_sem,
    send_sem,
    recv_sem,
    page_send_sem,
    page_recv_sem,
    back_sem,
    ret_sem,
):
    tokens, width = query_ref.shape
    length = recv.shape[0]
    heads = width // HD
    peers = length // tokens
    holders = lax.axis_size("exp")
    page_block = pages_out.shape[0] // holders
    seq, exp = lax.axis_index("seq"), lax.axis_index("exp")
    barrier = pltpu.get_barrier_semaphore()

    def seq_peer(i):
        return ((seq // SIDE + i // SIDE) % SIDE) * SIDE + (seq % SIDE + i % SIDE) % SIDE

    @pl.loop(1, peers)
    def _(i):
        pl.semaphore_signal(barrier, inc=1, device_id={"seq": seq_peer(i)}, device_id_type=MESH)

    @pl.loop(1, holders)
    def _(i):
        pl.semaphore_signal(
            barrier, inc=1, device_id={"exp": (exp + i) % holders}, device_id_type=MESH
        )

    load = pltpu.make_async_copy(w_out_hbm, w_out, weight_sem)
    load.start()

    own_lanes = pl.ds(pl.multiple_of(seq * tokens, tokens), tokens)
    segments = segment_ids_ref[...].astype(jnp.float32)
    segment_ref[...] = segments
    own_segment = jnp.broadcast_to(segment_ref[:, own_lanes], (tokens, tokens)).T[:, 0:1]
    own_index = seq * tokens + lax.broadcasted_iota(jnp.int32, (tokens, length), 0)
    index = lax.broadcasted_iota(jnp.int32, (tokens, length), 1)
    before = (segments == own_segment) & (index < own_index)
    positions = jnp.sum(jnp.where(before, 1.0, 0.0), axis=1, keepdims=True)
    lane = lax.broadcasted_iota(jnp.int32, (1, HD), 1)
    half = HD // 2
    power = (lane & (half - 1)).astype(jnp.float32) * (-math.log(theta_base) / half)
    angles = positions * jnp.exp(power)
    cosine_ref[...] = jnp.cos(angles)
    sine_ref[...] = jnp.sin(angles) * jnp.where(lane < half, -1.0, 1.0)

    def rotated(ref, cols):
        u = ref[:, cols].astype(jnp.float32)
        turned = pltpu.roll(u, HD // 2, 1)
        return (u * cosine_ref[...] + turned * sine_ref[...]).astype(jnp.bfloat16)

    @pl.loop(0, heads)
    def _(h):
        cols = pl.ds(pl.multiple_of(h * HD, HD), HD)
        value_cols = pl.ds(pl.multiple_of(width + h * HD, HD), HD)
        key_rot = rotated(key_ref, cols)
        value = value_ref[:, cols]
        send[h, :, 0:HD] = rotated(query_ref, cols)
        send[h, :, HD : 2 * HD] = key_rot
        send[h, :, 2 * HD : 3 * HD] = value
        page_rows[:, cols] = key_rot
        page_rows[:, value_cols] = value

    pl.semaphore_wait(barrier, peers - 1 + holders - 1)

    own_rows = pl.ds(pl.multiple_of(seq * tokens, tokens), tokens)
    own_cols = pl.ds(pl.multiple_of(seq * HD, HD), HD)

    @pl.loop(1, peers)
    def _(i):
        j = seq_peer(i)
        pltpu.make_async_remote_copy(
            src_ref=send.at[j],
            dst_ref=recv.at[own_rows],
            send_sem=send_sem,
            recv_sem=recv_sem,
            device_id={"seq": j},
            device_id_type=MESH,
        ).start()

    pltpu.make_async_copy(send.at[seq], recv.at[own_rows], recv_sem).start()

    page_total = holder_ref.shape[1]
    page_count = tokens // PAGE
    rows = pages_out.shape[0]
    own_holder = holder_ref[pl.ds(exp, 1), :].astype(jnp.float32)
    holder_col = jnp.broadcast_to(own_holder, (tokens, page_total)).T
    page_id = lax.broadcasted_iota(jnp.int32, (page_total, tokens), 0)
    token = lax.broadcasted_iota(jnp.int32, (page_total, tokens), 1)
    token_page = seq * page_count + token // PAGE
    holder_of = jnp.sum(
        jnp.where(page_id == token_page, holder_col, 0.0), axis=0, keepdims=True
    )
    ahead = (
        (holder_col == holder_of) & (page_id >= seq * page_count) & (page_id < token_page)
    )
    rank_of = jnp.sum(jnp.where(ahead, 1.0, 0.0), axis=0, keepdims=True)
    within = (lax.broadcasted_iota(jnp.int32, (1, tokens), 1) % PAGE).astype(jnp.float32)
    out_row = (holder_of * SEND_CAP + rank_of) * PAGE + within
    row_id = lax.broadcasted_iota(jnp.int32, (rows, tokens), 0).astype(jnp.float32)
    select = jnp.where(row_id == out_row, 1.0, 0.0).astype(jnp.bfloat16)

    @pl.loop(0, 2 * width // 512)
    def _(n):
        cols = pl.ds(pl.multiple_of(n * 512, 512), 512)
        pages_out[:, cols] = jnp.dot(
            select, page_rows[:, cols], preferred_element_type=jnp.float32
        ).astype(jnp.bfloat16)

    def page_slice(ref, holder):
        return ref.at[pl.ds(pl.multiple_of(holder * page_block, page_block), page_block)]

    @pl.loop(1, holders)
    def _(i):
        to = (exp + i) % holders
        pltpu.make_async_remote_copy(
            src_ref=page_slice(pages_out, to),
            dst_ref=page_slice(pages_in, exp),
            send_sem=page_send_sem,
            recv_sem=page_recv_sem,
            device_id={"exp": to},
            device_id_type=MESH,
        ).start()

    pltpu.make_async_copy(
        page_slice(pages_out, exp), page_slice(pages_in, exp), page_recv_sem
    ).start()

    packs = holder_ref.shape[0]
    page = lax.broadcasted_iota(jnp.int32, (packs, page_total), 1)
    ours = (
        (holder_ref[...] == exp)
        & (page >= seq * page_count)
        & (page < (seq + 1) * page_count)
    )
    ours_hot = jnp.where(ours, 1.0, 0.0)
    lower = lax.broadcasted_iota(jnp.int32, (page_total, page_total), 0)
    upper = lax.broadcasted_iota(jnp.int32, (page_total, page_total), 1)
    source_rank = jnp.dot(
        ours_hot.astype(jnp.bfloat16),
        jnp.where(lower < upper, 1.0, 0.0).astype(jnp.bfloat16),
        preferred_element_type=jnp.float32,
    )
    slots = slot_ref[...].astype(jnp.float32) + 1.0
    pack = lax.broadcasted_iota(jnp.int32, (packs, rows), 0)
    column = lax.broadcasted_iota(jnp.int32, (packs, rows), 1)
    slot_of = jnp.zeros((1, rows), jnp.float32)
    for rank in range(SEND_CAP):
        found = jnp.sum(
            jnp.where(source_rank == float(rank), ours_hot * slots, 0.0), axis=1, keepdims=True
        )
        mine = column // PAGE == pack * SEND_CAP + rank
        slot_of = slot_of + jnp.sum(jnp.where(mine, found, 0.0), axis=0, keepdims=True)
    inside = (lax.broadcasted_iota(jnp.int32, (1, rows), 1) % PAGE).astype(jnp.float32)
    cache_row = (slot_of - 1.0) * PAGE + inside
    cache_id = lax.broadcasted_iota(jnp.int32, (rows, rows), 0).astype(jnp.float32)
    placement_ref[...] = jnp.where(cache_id == cache_row, 1.0, 0.0).astype(jnp.bfloat16)

    pltpu.make_async_copy(recv, recv, recv_sem).wait()

    blocks = length // Q_ROWS
    window = Q_ROWS + REACH

    @pl.loop(0, blocks)
    def _(i):
        start = pl.multiple_of(((i + seq // 2) % blocks) * Q_ROWS, Q_ROWS)
        first = pl.multiple_of(jnp.maximum(start - REACH, 0), Q_ROWS)
        here = pl.ds(start, Q_ROWS)
        keys = pl.ds(first, window)
        scores = lax.dot_general(
            recv[here, 0:HD],
            recv[keys, HD : 2 * HD],
            (((1,), (1,)), ((), ())),
            preferred_element_type=jnp.float32,
        ) * (HD**-0.5)
        query_segment = jnp.broadcast_to(segment_ref[:, here], (HD, Q_ROWS)).T[:, 0:1]
        query_index = start + lax.broadcasted_iota(jnp.int32, (Q_ROWS, window), 0)
        key_index = first + lax.broadcasted_iota(jnp.int32, (Q_ROWS, window), 1)
        allowed = (key_index <= query_index) & (segment_ref[:, keys] == query_segment)
        scores = jnp.where(allowed, scores, -1e30)
        raised = jnp.exp(scores - jnp.max(scores, axis=-1, keepdims=True))
        weights = (raised * (1.0 / jnp.sum(raised, axis=-1, keepdims=True))).astype(jnp.bfloat16)
        mixed[here, :] = jnp.dot(
            weights, recv[keys, 2 * HD : 3 * HD], preferred_element_type=jnp.float32
        ).astype(jnp.bfloat16)
        for part in range(Q_ROWS // tokens):
            j = start // tokens + part
            rows = pl.ds(pl.multiple_of(j * tokens, tokens), tokens)

            @pl.when(j != seq)
            def _():
                pltpu.make_async_remote_copy(
                    src_ref=mixed.at[rows],
                    dst_ref=attn_rows.at[:, own_cols],
                    send_sem=back_sem,
                    recv_sem=ret_sem,
                    device_id={"seq": j},
                    device_id_type=MESH,
                ).start()

            @pl.when(j == seq)
            def _():
                pltpu.make_async_copy(mixed.at[rows], attn_rows.at[:, own_cols], ret_sem).start()

    load.wait()
    pltpu.make_async_copy(attn_rows, attn_rows, ret_sem).wait()

    @pl.loop(0, width // 512)
    def _(n):
        cols = pl.ds(pl.multiple_of(n * 512, 512), 512)
        hidden_ref[:, cols] = residual_ref[:, cols].astype(jnp.float32) + jnp.dot(
            attn_rows[...], w_out[:, cols], preferred_element_type=jnp.float32
        )

    pltpu.make_async_copy(pages_in, pages_in, page_recv_sem).wait()
    sent = send.at[pl.ds(0, peers - 1)]
    pltpu.make_async_copy(sent, sent, send_sem).wait()
    sent_back = mixed.at[pl.ds(0, length - tokens)]
    pltpu.make_async_copy(sent_back, sent_back, back_sem).wait()
    sent_pages = pages_out.at[pl.ds(0, page_block * (holders - 1))]
    pltpu.make_async_copy(sent_pages, sent_pages, page_send_sem).wait()


def run_front(query, key, value, residual, segments, page_holder, page_slot, w_out):
    tokens, width = query.shape
    length = segments.shape[1]
    heads = width // HD
    page_rows = page_holder.shape[0] * SEND_CAP * PAGE
    in_vmem = pl.BlockSpec(memory_space=pltpu.VMEM)
    in_hbm = pl.BlockSpec(memory_space=pl.ANY)
    return pl.pallas_call(
        front_kernel,
        out_shape=(
            jax.ShapeDtypeStruct((tokens, width), jnp.float32),
            jax.ShapeDtypeStruct((page_rows, page_rows), jnp.bfloat16),
            jax.ShapeDtypeStruct((page_rows, 2 * width), jnp.bfloat16),
        ),
        in_specs=[in_vmem] * 7 + [in_hbm],
        out_specs=(in_vmem, in_vmem, in_hbm),
        scratch_shapes=[
            pltpu.VMEM((heads, tokens, 3 * HD), jnp.bfloat16),
            pltpu.VMEM((length, 3 * HD), jnp.bfloat16),
            pltpu.VMEM((tokens, 2 * width), jnp.bfloat16),
            pltpu.VMEM((page_rows, 2 * width), jnp.bfloat16),
            pltpu.VMEM((length, HD), jnp.bfloat16),
            pltpu.VMEM((tokens, width), jnp.bfloat16),
            pltpu.VMEM(w_out.shape, jnp.bfloat16),
            pltpu.VMEM((1, length), jnp.float32),
            pltpu.VMEM((tokens, HD), jnp.float32),
            pltpu.VMEM((tokens, HD), jnp.float32),
        ]
        + [pltpu.SemaphoreType.DMA] * 7,
        compiler_params=pltpu.CompilerParams(
            collective_id=2, has_side_effects=True, vmem_limit_bytes=62 * 1024 * 1024
        ),
        name="front",
    )(query, key, value, residual, segments, page_holder, page_slot, w_out)


def shards(
    residual,
    query_heads,
    key_heads,
    value_heads,
    segment_ids,
    w_out,
    norm_gain,
    gate_scores,
    routes,
    w_gate,
    w_up,
    w_down,
    page_holder,
    page_slot,
):
    tok_rows = residual.shape[1]
    model_width = residual.shape[2]
    width = query_heads.shape[2]
    holders = lax.axis_size("exp")
    swap = [(i, i ^ 1) for i in range(holders)]
    own_half = (w_gate[0].T, w_up[0].T, w_down[0])
    other_half = tuple(lax.ppermute(part, "exp", swap) for part in own_half)
    hidden, placement, incoming = run_front(
        query_heads[0],
        key_heads[0],
        value_heads[0],
        residual[0],
        segment_ids,
        page_holder,
        page_slot,
        w_out,
    )
    kv_block = jnp.dot(placement, incoming, preferred_element_type=jnp.float32)
    kv_cache = kv_block.astype(jnp.bfloat16).reshape(1, holders * SEND_CAP, PAGE, 2 * width)
    layer_out = run_experts(
        hidden, norm_gain, gate_scores, routes, own_half, other_half
    ).reshape(1, tok_rows, model_width)
    return (layer_out, kv_cache)


def solution(mesh):
    placed = (
        P("exp", "seq", None),
        P("exp", "seq", None),
        P("exp", "seq", None),
        P("exp", "seq", None),
        P("exp", None),
        P(),
        P(),
        P("exp", "seq", None),
        P("exp", "seq", None),
        P(("seq", "exp"), None, None),
        P(("seq", "exp"), None, None),
        P(("seq", "exp"), None, None),
        P(),
        P(),
    )
    return jax.shard_map(
        shards,
        mesh=mesh,
        in_specs=placed,
        out_specs=(P("exp", "seq", None), P("seq", "exp", None, None)),
        check_vma=False,
    )
```

```python
import math

import jax
import jax.numpy as jnp
from jax import lax
from jax.experimental import pallas as pl
from jax.experimental.pallas import tpu as pltpu
from jax.sharding import PartitionSpec as P

HD = 128
TOP = 6
PAGE = 16
SEND_CAP = 2


theta_base = 10000.0
norm_eps = 1e-06
Q_ROWS = 256
REACH = 512


SIDE = 4
CHIPS = SIDE**3
GROUP = 16
GROUPS = CHIPS // GROUP
CAP = 16
MESH = pl.DeviceIdType.MESH


def offset_of(i):
    group, along_x, along_y = i // GROUP, (i // SIDE) % SIDE, i % SIDE
    return (group + along_x + along_y) % SIDE, along_x, along_y


def partner(i, backwards):
    seq, exp = lax.axis_index("seq"), lax.axis_index("exp")
    place = (seq // SIDE, seq % SIDE, exp // 2)
    step = offset_of(i)
    z, x, y = [
        (p + SIDE - d) % SIDE if backwards else (p + d) % SIDE for p, d in zip(place, step)
    ]
    return {"seq": z * SIDE + x, "exp": y * 2 + exp % 2}


def slot_experts(slots):
    seq, exp = lax.axis_index("seq"), lax.axis_index("exp")
    i = slots >> 4
    group, along_x, along_y = i >> 4, (i >> 2) & 3, i & 3
    z = (seq // SIDE + group + along_x + along_y) & 3
    x = (seq % SIDE + along_x) & 3
    y = (exp // 2 + along_y) & 3
    return (z * SIDE + x) * SIDE + y


def expert_kernel(
    hidden_ref,
    gain_ref,
    routes_ref,
    scores_ref,
    gate_own,
    up_own,
    down_own,
    gate_other,
    up_other,
    down_other,
    out_ref,
    send,
    recv,
    back,
    ret,
    gate_w,
    up_w,
    down_w,
    mix,
    total,
    weight_sem,
    send_sem,
    back_sem,
    recv_sem,
    ret_sem,
):
    tokens, width = hidden_ref.shape
    rows = GROUP * CAP
    slots = CHIPS * CAP
    barrier = pltpu.get_barrier_semaphore()

    @pl.loop(1, CHIPS)
    def _(i):
        pl.semaphore_signal(
            barrier, inc=1, device_id=partner(i, False), device_id_type=MESH
        )

    loads = []
    for part, (own, other, held) in enumerate(
        ((gate_own, gate_other, gate_w), (up_own, up_other, up_w), (down_own, down_other, down_w))
    ):
        for half, source in enumerate((own, other)):
            copy = pltpu.make_async_copy(source, held.at[half], weight_sem.at[part * 2 + half])
            copy.start()
            loads.append(copy)

    expert_ids = lax.broadcasted_iota(jnp.int32, (tokens, tokens), 0)
    token_ids = lax.broadcasted_iota(jnp.int32, (tokens, tokens), 1)
    scores = scores_ref[...]
    raised = jnp.exp(scores - jnp.max(scores, axis=0, keepdims=True))
    gates = raised / jnp.sum(raised, axis=0, keepdims=True)
    hits = jnp.zeros((tokens, tokens), jnp.float32)
    gate_of = jnp.zeros((tokens, tokens), jnp.float32)
    for k in range(TOP):
        hit = routes_ref[k] == expert_ids
        hits = hits + jnp.where(hit, 1.0, 0.0)
        gate_of = gate_of + jnp.where(hit, gates[k], 0.0)
    earlier = jnp.where(expert_ids < token_ids, 1.0, 0.0).astype(jnp.bfloat16)
    rank = jnp.dot(hits.astype(jnp.bfloat16), earlier, preferred_element_type=jnp.float32)
    rank1 = hits * (rank + 1.0)

    hidden = hidden_ref[...]
    mean_square = jnp.mean(hidden * hidden, axis=-1, keepdims=True)
    normed = (hidden * lax.rsqrt(mean_square + norm_eps) * gain_ref[...]).astype(jnp.bfloat16)
    rank1_narrow = rank1.astype(jnp.bfloat16)

    def block(ref, i):
        return ref.at[pl.ds(pl.multiple_of(i * CAP, CAP), CAP)]

    def build(g):
        slot = lax.broadcasted_iota(jnp.int32, (rows, tokens), 0) + g * rows
        expert = lax.broadcasted_iota(jnp.int32, (rows, tokens), 1)
        spread = jnp.where(slot_experts(slot) == expert, 1.0, 0.0).astype(jnp.bfloat16)
        found = jnp.dot(spread, rank1_narrow, preferred_element_type=jnp.float32)
        wanted = ((slot & (CAP - 1)) + 1).astype(jnp.float32)
        pick = jnp.where(found == wanted, 1.0, 0.0).astype(jnp.bfloat16)
        send[pl.ds(g * rows, rows), :] = jnp.dot(
            pick, normed, preferred_element_type=jnp.float32
        ).astype(jnp.bfloat16)

    def dispatch(g):
        @pl.loop(max(g * GROUP, 1), (g + 1) * GROUP)
        def _(i):
            pltpu.make_async_remote_copy(
                src_ref=block(send, i),
                dst_ref=block(recv, i),
                send_sem=send_sem,
                recv_sem=recv_sem.at[g],
                device_id=partner(i, False),
                device_id_type=MESH,
            ).start()

    build(0)
    pl.semaphore_wait(barrier, CHIPS - 1)
    dispatch(0)
    pltpu.make_async_copy(block(send, 0), block(recv, 0), recv_sem.at[0]).start()
    for g in range(1, GROUPS):
        build(g)
        if g > 1:
            dispatch(g - 1)

    rank1_rows = rank1.T.astype(jnp.bfloat16)
    gate_rows = gate_of.T.astype(jnp.bfloat16)
    for g in range(GROUPS):
        slot = lax.broadcasted_iota(jnp.int32, (tokens, rows), 1) + g * rows
        expert = lax.broadcasted_iota(jnp.int32, (tokens, rows), 0)
        spread = jnp.where(slot_experts(slot) == expert, 1.0, 0.0).astype(jnp.bfloat16)
        found = jnp.dot(rank1_rows, spread, preferred_element_type=jnp.float32)
        taken = jnp.dot(gate_rows, spread, preferred_element_type=jnp.float32)
        wanted = ((slot & (CAP - 1)) + 1).astype(jnp.float32)
        mix[:, g * rows : (g + 1) * rows] = jnp.where(found == wanted, taken, 0.0).astype(
            jnp.bfloat16
        )
        if g == 0:
            dispatch(GROUPS - 1)

    for copy in loads:
        copy.wait()

    across = (((1,), (1,)), ((), ()))

    @pl.loop(0, GROUPS)
    def _(g):
        here = pl.ds(pl.multiple_of(g * rows, rows), rows)
        pltpu.make_async_copy(recv.at[here], recv.at[here], recv_sem.at[g]).wait()
        for half in range(2):
            x = recv[here, :]
            gate = lax.dot_general(x, gate_w[half], across, preferred_element_type=jnp.float32)
            up = lax.dot_general(x, up_w[half], across, preferred_element_type=jnp.float32)
            active = (gate / (1.0 + jnp.exp(-gate)) * up).astype(jnp.bfloat16)
            down = jnp.dot(active, down_w[half], preferred_element_type=jnp.float32)
            if half == 0:
                total[...] = down
            else:
                back[here, :] = (total[...] + down).astype(jnp.bfloat16)

        @pl.loop(0, GROUP)
        def _(j):
            i = g * GROUP + j

            @pl.when(i > 0)
            def _():
                pltpu.make_async_remote_copy(
                    src_ref=block(back, i),
                    dst_ref=block(ret, i),
                    send_sem=back_sem,
                    recv_sem=ret_sem.at[g],
                    device_id=partner(i, True),
                    device_id_type=MESH,
                ).start()

            @pl.when(i == 0)
            def _():
                pltpu.make_async_copy(block(back, 0), block(ret, 0), ret_sem.at[0]).start()

    for g in range(GROUPS):
        here = pl.ds(g * rows, rows)
        pltpu.make_async_copy(ret.at[here], ret.at[here], ret_sem.at[g]).wait()
        part = jnp.dot(
            mix[:, g * rows : (g + 1) * rows], ret[here, :], preferred_element_type=jnp.float32
        )
        before = hidden_ref[...] if g == 0 else total[pl.ds(0, tokens), :]
        if g < GROUPS - 1:
            total[pl.ds(0, tokens), :] = before + part
        else:
            out_ref[...] = (before + part).astype(jnp.bfloat16)
    sent = pl.ds(CAP, slots - CAP)
    pltpu.make_async_copy(send.at[sent], send.at[sent], send_sem).wait()
    pltpu.make_async_copy(back.at[sent], back.at[sent], back_sem).wait()


def run_experts(hidden, norm_gain, scores, routes, own_half, other_half):
    tokens, width = hidden.shape
    half_ff = own_half[2].shape[0]
    slots = CHIPS * CAP
    in_vmem = pl.BlockSpec(memory_space=pltpu.VMEM)
    in_hbm = pl.BlockSpec(memory_space=pl.ANY)
    held = pltpu.VMEM((2, half_ff, width), jnp.bfloat16)
    buffer = pltpu.VMEM((slots, width), jnp.bfloat16)
    return pl.pallas_call(
        expert_kernel,
        out_shape=jax.ShapeDtypeStruct((tokens, width), jnp.bfloat16),
        in_specs=[in_vmem] * 4 + [in_hbm] * 6,
        out_specs=in_vmem,
        scratch_shapes=[
            buffer,
            buffer,
            buffer,
            buffer,
            held,
            held,
            held,
            pltpu.VMEM((tokens, slots), jnp.bfloat16),
            pltpu.VMEM((GROUP * CAP, width), jnp.float32),
            pltpu.SemaphoreType.DMA((6,)),
            pltpu.SemaphoreType.DMA,
            pltpu.SemaphoreType.DMA,
            pltpu.SemaphoreType.DMA((GROUPS,)),
            pltpu.SemaphoreType.DMA((GROUPS,)),
        ],
        compiler_params=pltpu.CompilerParams(
            collective_id=1, has_side_effects=True, vmem_limit_bytes=60 * 1024 * 1024
        ),
        name="experts",
    )(
        hidden,
        norm_gain[None, :],
        jnp.transpose(routes, (2, 0, 1)),
        jnp.transpose(scores, (2, 0, 1)),
        *own_half,
        *other_half,
    )


def front_kernel(
    query_hbm,
    key_hbm,
    value_hbm,
    residual_hbm,
    segment_ids_ref,
    holder_ref,
    slot_ref,
    w_out_hbm,
    hidden_ref,
    placement_ref,
    pages_in,
    send,
    recv,
    page_rows,
    pages_out,
    mixed,
    attn_rows,
    w_out,
    segment_ref,
    cosine_ref,
    sine_ref,
    query_ref,
    key_ref,
    value_ref,
    residual_ref,
    load_sem,
    weight_sem,
    send_sem,
    recv_sem,
    page_send_sem,
    page_recv_sem,
    back_sem,
    ret_sem,
):
    tokens, width = query_ref.shape
    length = recv.shape[0]
    heads = width // HD
    peers = length // tokens
    holders = lax.axis_size("exp")
    page_block = pages_out.shape[0] // holders
    seq, exp = lax.axis_index("seq"), lax.axis_index("exp")
    barrier = pltpu.get_barrier_semaphore()

    def seq_peer(i):
        return ((seq // SIDE + i // SIDE) % SIDE) * SIDE + (seq % SIDE + i % SIDE) % SIDE

    @pl.loop(1, peers)
    def _(i):
        pl.semaphore_signal(barrier, inc=1, device_id={"seq": seq_peer(i)}, device_id_type=MESH)

    @pl.loop(1, holders)
    def _(i):
        pl.semaphore_signal(
            barrier, inc=1, device_id={"exp": (exp + i) % holders}, device_id_type=MESH
        )

    loads = []
    for n, (source, held) in enumerate(
        (
            (query_hbm, query_ref),
            (key_hbm, key_ref),
            (value_hbm, value_ref),
            (residual_hbm, residual_ref),
        )
    ):
        copy = pltpu.make_async_copy(source, held, load_sem.at[n])
        copy.start()
        loads.append(copy)
    load = pltpu.make_async_copy(w_out_hbm, w_out, weight_sem)
    load.start()

    own_lanes = pl.ds(pl.multiple_of(seq * tokens, tokens), tokens)
    segments = segment_ids_ref[...].astype(jnp.float32)
    segment_ref[...] = segments
    own_segment = jnp.broadcast_to(segment_ref[:, own_lanes], (tokens, tokens)).T[:, 0:1]
    own_index = seq * tokens + lax.broadcasted_iota(jnp.int32, (tokens, length), 0)
    index = lax.broadcasted_iota(jnp.int32, (tokens, length), 1)
    before = (segments == own_segment) & (index < own_index)
    positions = jnp.sum(jnp.where(before, 1.0, 0.0), axis=1, keepdims=True)
    lane = lax.broadcasted_iota(jnp.int32, (1, HD), 1)
    half = HD // 2
    power = (lane & (half - 1)).astype(jnp.float32) * (-math.log(theta_base) / half)
    angles = positions * jnp.exp(power)
    cosine_ref[...] = jnp.cos(angles)
    sine_ref[...] = jnp.sin(angles) * jnp.where(lane < half, -1.0, 1.0)

    for copy in loads:
        copy.wait()

    def rotated(ref, cols):
        u = ref[:, cols].astype(jnp.float32)
        turned = pltpu.roll(u, HD // 2, 1)
        return (u * cosine_ref[...] + turned * sine_ref[...]).astype(jnp.bfloat16)

    @pl.loop(0, heads)
    def _(h):
        cols = pl.ds(pl.multiple_of(h * HD, HD), HD)
        value_cols = pl.ds(pl.multiple_of(width + h * HD, HD), HD)
        key_rot = rotated(key_ref, cols)
        value = value_ref[:, cols]
        send[h, :, 0:HD] = rotated(query_ref, cols)
        send[h, :, HD : 2 * HD] = key_rot
        send[h, :, 2 * HD : 3 * HD] = value
        page_rows[:, cols] = key_rot
        page_rows[:, value_cols] = value

    pl.semaphore_wait(barrier, peers - 1 + holders - 1)

    own_rows = pl.ds(pl.multiple_of(seq * tokens, tokens), tokens)
    own_cols = pl.ds(pl.multiple_of(seq * HD, HD), HD)

    @pl.loop(1, peers)
    def _(i):
        j = seq_peer(i)
        pltpu.make_async_remote_copy(
            src_ref=send.at[j],
            dst_ref=recv.at[own_rows],
            send_sem=send_sem,
            recv_sem=recv_sem,
            device_id={"seq": j},
            device_id_type=MESH,
        ).start()

    pltpu.make_async_copy(send.at[seq], recv.at[own_rows], recv_sem).start()

    page_total = holder_ref.shape[1]
    page_count = tokens // PAGE
    rows = pages_out.shape[0]
    own_holder = holder_ref[pl.ds(exp, 1), :].astype(jnp.float32)
    holder_col = jnp.broadcast_to(own_holder, (tokens, page_total)).T
    page_id = lax.broadcasted_iota(jnp.int32, (page_total, tokens), 0)
    token = lax.broadcasted_iota(jnp.int32, (page_total, tokens), 1)
    token_page = seq * page_count + token // PAGE
    holder_of = jnp.sum(
        jnp.where(page_id == token_page, holder_col, 0.0), axis=0, keepdims=True
    )
    ahead = (
        (holder_col == holder_of) & (page_id >= seq * page_count) & (page_id < token_page)
    )
    rank_of = jnp.sum(jnp.where(ahead, 1.0, 0.0), axis=0, keepdims=True)
    within = (lax.broadcasted_iota(jnp.int32, (1, tokens), 1) % PAGE).astype(jnp.float32)
    out_row = (holder_of * SEND_CAP + rank_of) * PAGE + within
    row_id = lax.broadcasted_iota(jnp.int32, (rows, tokens), 0).astype(jnp.float32)
    select = jnp.where(row_id == out_row, 1.0, 0.0).astype(jnp.bfloat16)

    @pl.loop(0, 2 * width // 512)
    def _(n):
        cols = pl.ds(pl.multiple_of(n * 512, 512), 512)
        pages_out[:, cols] = jnp.dot(
            select, page_rows[:, cols], preferred_element_type=jnp.float32
        ).astype(jnp.bfloat16)

    def page_slice(ref, holder):
        return ref.at[pl.ds(pl.multiple_of(holder * page_block, page_block), page_block)]

    @pl.loop(1, holders)
    def _(i):
        to = (exp + i) % holders
        pltpu.make_async_remote_copy(
            src_ref=page_slice(pages_out, to),
            dst_ref=page_slice(pages_in, exp),
            send_sem=page_send_sem,
            recv_sem=page_recv_sem,
            device_id={"exp": to},
            device_id_type=MESH,
        ).start()

    pltpu.make_async_copy(
        page_slice(pages_out, exp), page_slice(pages_in, exp), page_recv_sem
    ).start()

    packs = holder_ref.shape[0]
    page = lax.broadcasted_iota(jnp.int32, (packs, page_total), 1)
    ours = (
        (holder_ref[...] == exp)
        & (page >= seq * page_count)
        & (page < (seq + 1) * page_count)
    )
    ours_hot = jnp.where(ours, 1.0, 0.0)
    lower = lax.broadcasted_iota(jnp.int32, (page_total, page_total), 0)
    upper = lax.broadcasted_iota(jnp.int32, (page_total, page_total), 1)
    source_rank = jnp.dot(
        ours_hot.astype(jnp.bfloat16),
        jnp.where(lower < upper, 1.0, 0.0).astype(jnp.bfloat16),
        preferred_element_type=jnp.float32,
    )
    slots = slot_ref[...].astype(jnp.float32) + 1.0
    pack = lax.broadcasted_iota(jnp.int32, (packs, rows), 0)
    column = lax.broadcasted_iota(jnp.int32, (packs, rows), 1)
    slot_of = jnp.zeros((1, rows), jnp.float32)
    for rank in range(SEND_CAP):
        found = jnp.sum(
            jnp.where(source_rank == float(rank), ours_hot * slots, 0.0), axis=1, keepdims=True
        )
        mine = column // PAGE == pack * SEND_CAP + rank
        slot_of = slot_of + jnp.sum(jnp.where(mine, found, 0.0), axis=0, keepdims=True)
    inside = (lax.broadcasted_iota(jnp.int32, (1, rows), 1) % PAGE).astype(jnp.float32)
    cache_row = (slot_of - 1.0) * PAGE + inside
    cache_id = lax.broadcasted_iota(jnp.int32, (rows, rows), 0).astype(jnp.float32)
    placement_ref[...] = jnp.where(cache_id == cache_row, 1.0, 0.0).astype(jnp.bfloat16)

    pltpu.make_async_copy(recv, recv, recv_sem).wait()

    blocks = length // Q_ROWS
    window = Q_ROWS + REACH

    @pl.loop(0, blocks)
    def _(i):
        start = pl.multiple_of(((i + seq // 2) % blocks) * Q_ROWS, Q_ROWS)
        first = pl.multiple_of(jnp.maximum(start - REACH, 0), Q_ROWS)
        here = pl.ds(start, Q_ROWS)
        keys = pl.ds(first, window)
        scores = lax.dot_general(
            recv[here, 0:HD],
            recv[keys, HD : 2 * HD],
            (((1,), (1,)), ((), ())),
            preferred_element_type=jnp.float32,
        ) * (HD**-0.5)
        query_segment = jnp.broadcast_to(segment_ref[:, here], (HD, Q_ROWS)).T[:, 0:1]
        query_index = start + lax.broadcasted_iota(jnp.int32, (Q_ROWS, window), 0)
        key_index = first + lax.broadcasted_iota(jnp.int32, (Q_ROWS, window), 1)
        allowed = (key_index <= query_index) & (segment_ref[:, keys] == query_segment)
        scores = jnp.where(allowed, scores, -1e30)
        raised = jnp.exp(scores - jnp.max(scores, axis=-1, keepdims=True))
        weights = (raised * (1.0 / jnp.sum(raised, axis=-1, keepdims=True))).astype(jnp.bfloat16)
        mixed[here, :] = jnp.dot(
            weights, recv[keys, 2 * HD : 3 * HD], preferred_element_type=jnp.float32
        ).astype(jnp.bfloat16)
        for part in range(Q_ROWS // tokens):
            j = start // tokens + part
            rows = pl.ds(pl.multiple_of(j * tokens, tokens), tokens)

            @pl.when(j != seq)
            def _():
                pltpu.make_async_remote_copy(
                    src_ref=mixed.at[rows],
                    dst_ref=attn_rows.at[:, own_cols],
                    send_sem=back_sem,
                    recv_sem=ret_sem,
                    device_id={"seq": j},
                    device_id_type=MESH,
                ).start()

            @pl.when(j == seq)
            def _():
                pltpu.make_async_copy(mixed.at[rows], attn_rows.at[:, own_cols], ret_sem).start()

    load.wait()
    pltpu.make_async_copy(attn_rows, attn_rows, ret_sem).wait()

    @pl.loop(0, width // 512)
    def _(n):
        cols = pl.ds(pl.multiple_of(n * 512, 512), 512)
        hidden_ref[:, cols] = residual_ref[:, cols].astype(jnp.float32) + jnp.dot(
            attn_rows[...], w_out[:, cols], preferred_element_type=jnp.float32
        )

    pltpu.make_async_copy(pages_in, pages_in, page_recv_sem).wait()
    sent = send.at[pl.ds(0, peers - 1)]
    pltpu.make_async_copy(sent, sent, send_sem).wait()
    sent_back = mixed.at[pl.ds(0, length - tokens)]
    pltpu.make_async_copy(sent_back, sent_back, back_sem).wait()
    sent_pages = pages_out.at[pl.ds(0, page_block * (holders - 1))]
    pltpu.make_async_copy(sent_pages, sent_pages, page_send_sem).wait()


def run_front(query, key, value, residual, segments, page_holder, page_slot, w_out):
    tokens, width = query.shape
    length = segments.shape[1]
    heads = width // HD
    page_rows = page_holder.shape[0] * SEND_CAP * PAGE
    in_vmem = pl.BlockSpec(memory_space=pltpu.VMEM)
    in_hbm = pl.BlockSpec(memory_space=pl.ANY)
    return pl.pallas_call(
        front_kernel,
        out_shape=(
            jax.ShapeDtypeStruct((tokens, width), jnp.float32),
            jax.ShapeDtypeStruct((page_rows, page_rows), jnp.bfloat16),
            jax.ShapeDtypeStruct((page_rows, 2 * width), jnp.bfloat16),
        ),
        in_specs=[in_hbm] * 4 + [in_vmem] * 3 + [in_hbm],
        out_specs=(in_vmem, in_vmem, in_hbm),
        scratch_shapes=[
            pltpu.VMEM((heads, tokens, 3 * HD), jnp.bfloat16),
            pltpu.VMEM((length, 3 * HD), jnp.bfloat16),
            pltpu.VMEM((tokens, 2 * width), jnp.bfloat16),
            pltpu.VMEM((page_rows, 2 * width), jnp.bfloat16),
            pltpu.VMEM((length, HD), jnp.bfloat16),
            pltpu.VMEM((tokens, width), jnp.bfloat16),
            pltpu.VMEM(w_out.shape, jnp.bfloat16),
            pltpu.VMEM((1, length), jnp.float32),
            pltpu.VMEM((tokens, HD), jnp.float32),
            pltpu.VMEM((tokens, HD), jnp.float32),
        ]
        + [pltpu.VMEM((tokens, width), jnp.bfloat16)] * 4
        + [pltpu.SemaphoreType.DMA((4,))]
        + [pltpu.SemaphoreType.DMA] * 7,
        compiler_params=pltpu.CompilerParams(
            collective_id=2, has_side_effects=True, vmem_limit_bytes=62 * 1024 * 1024
        ),
        name="front",
    )(query, key, value, residual, segments, page_holder, page_slot, w_out)


def shards(
    residual,
    query_heads,
    key_heads,
    value_heads,
    segment_ids,
    w_out,
    norm_gain,
    gate_scores,
    routes,
    w_gate,
    w_up,
    w_down,
    page_holder,
    page_slot,
):
    tok_rows = residual.shape[1]
    model_width = residual.shape[2]
    width = query_heads.shape[2]
    holders = lax.axis_size("exp")
    swap = [(i, i ^ 1) for i in range(holders)]
    own_half = (w_gate[0].T, w_up[0].T, w_down[0])
    other_half = tuple(lax.ppermute(part, "exp", swap) for part in own_half)
    hidden, placement, incoming = run_front(
        query_heads[0],
        key_heads[0],
        value_heads[0],
        residual[0],
        segment_ids,
        page_holder,
        page_slot,
        w_out,
    )
    kv_block = jnp.dot(placement, incoming, preferred_element_type=jnp.float32)
    kv_cache = kv_block.astype(jnp.bfloat16).reshape(1, holders * SEND_CAP, PAGE, 2 * width)
    layer_out = run_experts(
        hidden, norm_gain, gate_scores, routes, own_half, other_half
    ).reshape(1, tok_rows, model_width)
    return (layer_out, kv_cache)


def solution(mesh):
    placed = (
        P("exp", "seq", None),
        P("exp", "seq", None),
        P("exp", "seq", None),
        P("exp", "seq", None),
        P("exp", None),
        P(),
        P(),
        P("exp", "seq", None),
        P("exp", "seq", None),
        P(("seq", "exp"), None, None),
        P(("seq", "exp"), None, None),
        P(("seq", "exp"), None, None),
        P(),
        P(),
    )
    return jax.shard_map(
        shards,
        mesh=mesh,
        in_specs=placed,
        out_specs=(P("exp", "seq", None), P("seq", "exp", None, None)),
        check_vma=False,
    )
```
